128 devices in a mesh: wide: 32 (over z, y, core), narrow: 4 (over x).
Axes of the slice: x: 4, y: 4, z: 4, core: 2. Of those that a mesh axis runs over, the one named last changes fastest.
Arguments:
- resid: bfloat16 [512, 16384], P(('wide', 'narrow')), may hold values from -6 to 6
- queries: bfloat16 [512, 16384], P(('wide', 'narrow')), may hold values from -9 to 9
- key_cache: bfloat16 [512, 192, 1024], P(('wide', 'narrow')), may hold values from -4 to 4
- value_cache: bfloat16 [512, 192, 1024], P(('wide', 'narrow')), may hold values from -6 to 6
- new_keys: bfloat16 [512, 1024], P(('wide', 'narrow')), may hold values from -4 to 4
- new_values: bfloat16 [512, 1024], P(('wide', 'narrow')), may hold values from -6 to 6
- lengths: int32 [512], P(('wide', 'narrow')), may hold values from 2 to 192, as said below
- norm_gain: bfloat16 [16384], replicated, may hold values from 0.099609375 to 1.8984375
- w_gate: bfloat16 [16384, 28672], P('narrow', 'wide'), may hold values from -0.046875 to 0.046875
- w_up: bfloat16 [16384, 28672], P('narrow', 'wide'), may hold values from -0.046875 to 0.046875
- w_down: bfloat16 [28672, 16384], P('wide', 'narrow'), may hold values from -0.03125 to 0.03125
Outputs:
- layer_out: bfloat16 [512, 16384], P(('wide', 'narrow'))
The draws below stay inside these ranges and needn't reach their ends.
Inputs may be any that keep to these rules, and one draw needn't show every extreme that they name: Positions below lengths[b] of sequence b are live; some sequence holds all 192.
All inputs are finite; a program needn't handle non-finite values.
Results may differ from the reference program's by a relative error of at most 0.019.
Values may be sent and summed in bfloat16 or wider, within the bound.
A program may use at most 128 MiB of HBM per device.

```python
import jax
import jax.numpy as jnp
from jax import lax

CACHE = 192
D = 16384
FF = 28672
HEADS = 128
KVH = 8
HD = 128
BATCH = 512
N_WIDE = 32
N_NARROW = 4


def draw_queries(key, part):
    columns = HEADS * HD
    values = jnp.clip(jax.random.normal(key, (BATCH, columns), jnp.float32), -6.0, 6.0)
    return values.astype(jnp.bfloat16)


def draw_key_cache(key, part):
    columns = KVH * HD
    values = jnp.clip(jax.random.normal(key, (BATCH, CACHE, columns), jnp.float32), -4.0, 4.0)
    return values.astype(jnp.bfloat16)


def draw_lengths(key, part):
    drawn = jax.random.randint(key, (BATCH,), 2, CACHE + 1, dtype=jnp.int32)
    where_full = jax.random.randint(jax.random.fold_in(key, 11), (), 0, BATCH, dtype=jnp.int32)
    return drawn.at[where_full].set(CACHE)


def shard_levels(own_key, shape, split, least, largest):
    level = 1.0
    for axis_at, blocks in split:
        heights = jax.random.uniform(jax.random.fold_in(jax.random.fold_in(own_key, 6), axis_at), (blocks,), jnp.float32, least / len(split), largest / len(split))
        level = level * jnp.repeat(jnp.exp(heights), shape[axis_at] // blocks).reshape((-1,) + (1,) * (len(shape) - 1 - axis_at))
    return level


def gaussian(own_key, shape, scale, reach, cuts=(), held_as=jnp.bfloat16):
    loudness = shard_levels(own_key, shape, cuts, -0.22, 0.18) if cuts else 1.0
    array = jax.random.normal(own_key, shape, jnp.float32) * scale * loudness
    return jnp.minimum(jnp.maximum(array, -reach), reach).astype(held_as)


def setup_inputs(seed: int = 0) -> dict:
    splits = jax.random.split(jax.random.key(seed), 12)
    resid = gaussian(splits[0], (BATCH, D), 1.0, 6.0, ((0, 128),))
    queries = draw_queries(jax.random.fold_in(splits[11], 71), 0)
    key_cache = draw_key_cache(jax.random.fold_in(splits[11], 71), 0)
    value_cache = gaussian(splits[3], (BATCH, CACHE, KVH * HD), 1.0, 6.0, ((0, 128),))
    new_keys = gaussian(splits[4], (BATCH, KVH * HD), 1.0, 4.0, ((0, 128),))
    new_values = gaussian(splits[5], (BATCH, KVH * HD), 1.0, 6.0, ((0, 128),))
    lengths = draw_lengths(jax.random.fold_in(splits[11], 71), 0)
    norm_gain = jnp.clip(1.0 + 0.18 * jax.random.normal(splits[7], (D,), jnp.float32), 0.099609375, 1.8984375).astype(jnp.bfloat16)
    w_gate = gaussian(splits[8], (D, FF), D ** -0.5, 0.046875, ((0, 4), (1, 32)))
    w_up = gaussian(splits[9], (D, FF), D ** -0.5, 0.046875, ((0, 4), (1, 32)))
    w_down = gaussian(splits[10], (FF, D), FF ** -0.5, 0.03125, ((0, 32), (1, 4)))
    return {"resid": resid, "queries": queries, "key_cache": key_cache, "value_cache": value_cache, "new_keys": new_keys, "new_values": new_values, "lengths": lengths, "norm_gain": norm_gain, "w_gate": w_gate, "w_up": w_up, "w_down": w_down}


def attend(query_rows, key_rows, value_rows, key_new, value_new, length_rows):
    count = query_rows.shape[0]
    groups = HEADS // KVH
    qh = query_rows.reshape(count, KVH, groups, HD).astype(jnp.float32)
    kh = key_rows.reshape(count, CACHE, KVH, HD).astype(jnp.float32)
    vh = value_rows.reshape(count, CACHE, KVH, HD).astype(jnp.float32)
    kn = key_new.reshape(count, KVH, HD).astype(jnp.float32)
    vn = value_new.reshape(count, KVH, HD).astype(jnp.float32)
    score_scale = 1.0 / HD ** 0.5
    scores = jnp.einsum('bgqd,btgd->bgqt', qh, kh) * score_scale
    own = jnp.einsum('bgqd,bgd->bgq', qh, kn) * score_scale
    live = jnp.arange(CACHE, dtype=jnp.int32)[None, :] < length_rows[:, None]
    live = live[:, None, None, :]
    scores = jnp.where(live, scores, jnp.float32(-1e+30))
    row_top = jnp.maximum(lax.optimization_barrier(jnp.max(scores, axis=-1)), own)
    cache_exp = jnp.where(live, jnp.exp(scores - row_top[..., None]), jnp.float32(0.0))
    own_exp = jnp.exp(own - row_top)
    total = lax.optimization_barrier(jnp.sum(cache_exp, axis=-1)) + own_exp
    probs = (cache_exp / total[..., None]).astype(jnp.bfloat16)
    own_prob = (own_exp / total).astype(jnp.bfloat16)
    attended = jnp.einsum('bgqt,btgd->bgqd', probs.astype(jnp.float32), vh)
    attended = attended + own_prob.astype(jnp.float32)[..., None] * vn[:, :, None, :]
    return attended.reshape(count, HEADS * HD)

def blocked_product(left, right, blocks):
    width = left.shape[1] // blocks
    total = jnp.zeros((left.shape[0], right.shape[1]), jnp.float32)
    for block in range(blocks):
        term = jnp.dot(left[:, block * width:(block + 1) * width], right[block * width:(block + 1) * width], preferred_element_type=jnp.float32)
        total = total + term.astype(jnp.bfloat16).astype(jnp.float32)
    return total

def reference(resid, queries, key_cache, value_cache, new_keys, new_values, lengths, norm_gain, w_gate, w_up, w_down):

    def single(items):
        picked = [item[None] for item in items]
        return attend(*picked)[0]
    attended = lax.map(single, (queries, key_cache, value_cache, new_keys, new_values, lengths))
    mixed = resid.astype(jnp.float32) + attended
    mean_square = lax.optimization_barrier(jnp.mean(mixed * mixed, axis=-1, keepdims=True))
    normed = (mixed * lax.rsqrt(mean_square + 1e-05) * norm_gain.astype(jnp.float32)).astype(jnp.bfloat16)
    gate = blocked_product(normed, w_gate, N_NARROW)
    up_rows = blocked_product(normed, w_up, N_NARROW)
    hidden = (jax.nn.silu(gate) * up_rows).astype(jnp.bfloat16)
    ffn_out = blocked_product(hidden, w_down, N_WIDE).astype(jnp.bfloat16)
    return (mixed + ffn_out.astype(jnp.float32)).astype(jnp.bfloat16)
```

```python
import functools

import jax
import jax.numpy as jnp
from jax import lax
from jax.experimental import pallas as pl
from jax.experimental.pallas import tpu as pltpu
from jax.sharding import PartitionSpec as P

HEADS = 128
KVH = 8
HD = 128
MESH = pl.DeviceIdType.MESH
F32 = jnp.float32
BF16 = jnp.bfloat16
COPIES = 112


def attend(query_rows, key_rows, value_rows, key_new, value_new, length_rows):
    count = query_rows.shape[0]
    cached = key_rows.shape[1]
    groups = HEADS // KVH
    qh = query_rows.reshape(count, KVH, groups, HD)
    kh = key_rows.reshape(count, cached, KVH, HD)
    vh = value_rows.reshape(count, cached, KVH, HD)
    kn = key_new.reshape(count, KVH, HD)
    vn = value_new.reshape(count, KVH, HD)
    score_scale = 1.0 / HD**0.5
    scores = jnp.einsum("bgqd,btgd->bgqt", qh, kh, preferred_element_type=jnp.float32) * score_scale
    own = jnp.einsum("bgqd,bgd->bgq", qh, kn, preferred_element_type=jnp.float32) * score_scale
    live = jnp.arange(cached, dtype=jnp.int32)[None, :] < length_rows[:, None]
    live = live[:, None, None, :]
    scores = jnp.where(live, scores, jnp.float32(-1e30))
    row_top = jnp.maximum(jnp.max(scores, axis=-1), own)
    cache_exp = jnp.where(live, jnp.exp(scores - row_top[..., None]), jnp.float32(0.0))
    own_exp = jnp.exp(own - row_top)
    total = jnp.sum(cache_exp, axis=-1) + own_exp
    probs = (cache_exp / total[..., None]).astype(jnp.bfloat16)
    own_prob = (own_exp / total).astype(jnp.bfloat16)
    attended = jnp.einsum("bgqt,btgd->bgqd", probs, vh, preferred_element_type=jnp.float32)
    attended = (
        attended + own_prob.astype(jnp.float32)[..., None] * vn.astype(jnp.float32)[:, :, None, :]
    )
    return attended.reshape(count, HEADS * HD)


def ffn_kernel(
    nrm, wg_hbm, wu_hbm, wd_hbm,
    out,
    wgu, wd, abuf, stage, x_all,
    part, ra, rb, rm, rp, hid,
    dpart, sib, ya, yb, ym, yp, zs, zr, fb, gather,
    wsem, osem, ss, rs,
):
    x = lax.axis_index("narrow")
    w = lax.axis_index("wide")
    z = lax.div(w, 8)
    y = lax.rem(lax.div(w, 2), 4)
    core = lax.rem(w, 2)

    def wrap(v):
        return lax.rem(v + 4, 4)

    def X(d):
        return {"narrow": wrap(x + d)}

    def Y(d):
        return {"wide": z * 8 + wrap(y + d) * 2 + core}

    def Z(d):
        return {"wide": wrap(z + d) * 8 + y * 2 + core}

    other = 1 - core
    S = {"wide": w + 1 - 2 * core}

    count = [0]
    started = []

    def rc(src, dst, dev):
        i = count[0]
        count[0] += 1
        c = pltpu.make_async_remote_copy(
            src_ref=src, dst_ref=dst, send_sem=ss.at[i], recv_sem=rs.at[i],
            device_id=dev, device_id_type=MESH)
        started.append(c)
        c.start()
        return c

    loads = []
    hid_tiles = wgu.shape[0]
    down_tiles = wd.shape[0]
    dn = wd.shape[2]
    for j in range(hid_tiles):
        for k, src in enumerate((wg_hbm, wu_hbm)):
            loads.append(pltpu.make_async_copy(
                src.at[:, pl.ds(j * 128, 128)], wgu.at[j, :, pl.ds(k * 128, 128)], wsem.at[j, k]))
    dloads = []
    for n in range(down_tiles):
        dloads.append(pltpu.make_async_copy(
            wd_hbm.at[:, pl.ds(n * dn, dn)], wd.at[n], wsem.at[hid_tiles + n, 0]))
    for c in loads:
        c.start()
    for c in dloads:
        c.start()

    barrier = pltpu.get_barrier_semaphore()
    peers = [X(1), X(2), X(3), Y(1), Y(3), Z(1), Z(2), Z(3), S]
    for p in peers:
        pl.semaphore_signal(barrier, inc=1, device_id=p, device_id_type=MESH)
    pl.semaphore_wait(barrier, len(peers))

    a2a = [rc(nrm.at[wrap(x + d)], abuf.at[x], X(d)) for d in (1, 2, 3)]
    keep = pltpu.make_async_copy(nrm.at[x], abuf.at[x], osem.at[0])
    keep.start()
    keep.wait()
    for c in a2a:
        c.wait_recv()
    for q in range(4):
        stage[pl.ds(4 * q, 4), :] = abuf[q].astype(F32)
    x_all[z, core, y] = stage[...].astype(BF16)

    rel = (0, -1, 1, 2)
    zcopies = {}
    scopies = []

    def block(dz, dy):
        return x_all.at[wrap(z + dz), core, wrap(y + dy)]

    def spread(r):
        b = block(0, r)
        for d in (1, -1):
            zcopies[(d, r)] = rc(b, b, Z(d))
        scopies.append(rc(b, b, S))

    b0 = block(0, 0)
    yplus = rc(b0, b0, Y(1))
    yminus = rc(b0, b0, Y(-1))
    spread(0)
    half = x_all.shape[4] // 2
    yplus.wait_recv()
    fa = block(0, -1).at[:, pl.ds(0, half)]
    f0 = rc(fa, fa, Y(1))
    yminus.wait_recv()
    fbk = block(0, 1).at[:, pl.ds(half, half)]
    f1 = rc(fbk, fbk, Y(-1))
    spread(-1)
    spread(1)
    f0.wait_recv()
    f1.wait_recv()
    spread(2)
    for c in scopies:
        c.wait_recv()

    deltas = (0, 1, -1, 2)
    slabs = {}
    fwd = []

    def slab_to_sibling(k):
        b = x_all.at[wrap(z + deltas[k]), core]
        slabs[k] = rc(b, b, S)

    def z_arrive():
        for r in (0, -1):
            zcopies[(1, r)].wait_recv()
            b = block(-1, r)
            fwd.append(rc(b, b, Z(1)))
        zcopies[(-1, 0)].wait_recv()
        zcopies[(-1, -1)].wait_recv()
        for r in (1, 2):
            zcopies[(-1, r)].wait_recv()
            b = block(1, r)
            fwd.append(rc(b, b, Z(-1)))
        slab_to_sibling(1)
        zcopies[(1, 1)].wait_recv()
        zcopies[(1, 2)].wait_recv()
        slab_to_sibling(2)

    def z_last():
        for c in fwd:
            c.wait_recv()
        slab_to_sibling(3)

    rsx = {}

    def gate_up(k):
        if k > 0:
            slabs[k].wait_recv()
        zi = wrap(z + deltas[k])
        rows = 128

        def step(j, carry):
            lhs = x_all[zi].reshape(rows, x_all.shape[4])
            r = jnp.dot(lhs, wgu[j], preferred_element_type=F32).astype(BF16)
            part[k, :, :, :, pl.ds(pl.multiple_of(j * 256, 256), 256)] = r.reshape(4, 2, 16, 256)
            return carry

        lax.fori_loop(0, hid_tiles, step, 0)
        xp1, xm1, xp2 = wrap(x + 1), wrap(x - 1), wrap(x + 2)
        rsx[k] = [
            rc(part.at[k, xp2, 0], ra.at[k], X(1)),
            rc(part.at[k, xp2, 1], rb.at[k], X(-1)),
            rc(part.at[k, xp1, 1], rm.at[k, 1], X(1)),
            rc(part.at[k, xm1, 0], rp.at[k, 0], X(-1)),
        ]

    def reduce_mid(k):
        xp1, xm1 = wrap(x + 1), wrap(x - 1)
        rsx[k][0].wait_recv()
        part[k, xp1, 0] = (part[k, xp1, 0].astype(F32) + ra[k].astype(F32)).astype(BF16)
        rsx[k].append(rc(part.at[k, xp1, 0], rm.at[k, 0], X(1)))
        rsx[k][1].wait_recv()
        part[k, xm1, 1] = (part[k, xm1, 1].astype(F32) + rb[k].astype(F32)).astype(BF16)
        rsx[k].append(rc(part.at[k, xm1, 1], rp.at[k, 1], X(-1)))

    hcopies = {}

    def gate(k):
        for c in rsx[k][2:]:
            c.wait_recv()
        for j in range(hid_tiles):
            g = pl.ds(j * 256, 128)
            u = pl.ds(j * 256 + 128, 128)

            def total(cols):
                return (part[k, x, :, :, cols].astype(F32) + rm[k, :, :, cols].astype(F32)
                        + rp[k, :, :, cols].astype(F32))

            hid[k, x, :, :, pl.ds(j * 128, 128)] = (jax.nn.silu(total(g)) * total(u)).astype(BF16)
        b = hid.at[k, x]
        hcopies[k] = [rc(b, b, X(1)), rc(b, b, X(-1))]

    def hid_forward(k):
        hcopies[k][0].wait_recv()
        b = hid.at[k, wrap(x - 1), 0]
        hcopies[k].append(rc(b, b, X(1)))
        hcopies[k][1].wait_recv()
        b = hid.at[k, wrap(x + 1), 1]
        hcopies[k].append(rc(b, b, X(-1)))

    ecopies = {}

    def down(k):
        for c in hcopies[k][2:]:
            c.wait_recv()

        def step(n, carry):
            lhs = hid[k].reshape(128, hid.shape[4])
            r = jnp.dot(lhs, wd[n], preferred_element_type=F32).astype(BF16)
            dpart[k, :, :, :, pl.ds(pl.multiple_of(n * dn, dn), dn)] = r.reshape(2, 4, 16, dn)
            return carry

        lax.fori_loop(0, down_tiles, step, 0)
        ecopies[k] = rc(dpart.at[k, other], sib.at[k], S)

    lo = pl.ds(0, half)
    hi = pl.ds(half, half)
    rsy = {}

    def sib_add(k):
        ecopies[k].wait_recv()
        yp1, ym1, yp2 = wrap(y + 1), wrap(y - 1), wrap(y + 2)

        def step(i, carry):
            yi = lax.rem(yp2 + i, 4)
            dpart[k, core, yi] = (dpart[k, core, yi].astype(F32) + sib[k, yi].astype(F32)).astype(BF16)
            return carry

        lax.fori_loop(0, 4, step, 0)
        rsy[k] = [
            rc(dpart.at[k, core, yp2, :, lo], ya.at[k], Y(1)),
            rc(dpart.at[k, core, yp2, :, hi], yb.at[k], Y(-1)),
            rc(dpart.at[k, core, yp1, :, hi], ym.at[k, :, hi], Y(1)),
            rc(dpart.at[k, core, ym1, :, lo], yp.at[k, :, lo], Y(-1)),
        ]

    def y_mid(k):
        yp1, ym1 = wrap(y + 1), wrap(y - 1)
        rsy[k][0].wait_recv()
        dpart[k, core, yp1, :, lo] = (dpart[k, core, yp1, :, lo].astype(F32) + ya[k].astype(F32)).astype(BF16)
        rsy[k].append(rc(dpart.at[k, core, yp1, :, lo], ym.at[k, :, lo], Y(1)))
        rsy[k][1].wait_recv()
        dpart[k, core, ym1, :, hi] = (dpart[k, core, ym1, :, hi].astype(F32) + yb[k].astype(F32)).astype(BF16)
        rsy[k].append(rc(dpart.at[k, core, ym1, :, hi], yp.at[k, :, hi], Y(-1)))

    zsum = {}

    def y_fin(k):
        for c in rsy[k][2:]:
            c.wait_recv()
        t = dpart[k, core, y].astype(F32) + ym[k].astype(F32) + yp[k].astype(F32)
        if k == 0:
            stage[...] = t
        else:
            zs[k] = t.astype(BF16)
            zsum[k] = rc(zs.at[k], zr.at[k], Z(deltas[k]))

    def finish():
        for k in (1, 2, 3):
            zsum[k].wait_recv()
        stage[...] = (stage[...] + zr[1].astype(F32) + zr[2].astype(F32) + zr[3].astype(F32))
        for q in range(4):
            fb[q] = stage[pl.ds(4 * q, 4), :].astype(BF16)
        back = [rc(fb.at[wrap(x + d)], gather.at[x], X(d)) for d in (1, 2, 3)]
        keep = pltpu.make_async_copy(fb.at[x], gather.at[x], osem.at[1])
        keep.start()
        keep.wait()
        for c in back:
            c.wait_recv()
        out[...] = gather[...]

    for c in loads:
        c.wait()
    gate_up(0)
    reduce_mid(0)
    gate(0)
    hid_forward(0)
    z_arrive()
    for c in dloads:
        c.wait()
    down(0)
    gate_up(1)
    sib_add(0)
    gate_up(2)
    reduce_mid(1)
    y_mid(0)
    z_last()
    gate(1)
    reduce_mid(2)
    hid_forward(1)
    gate(2)
    gate_up(3)
    y_fin(0)
    hid_forward(2)
    down(1)
    reduce_mid(3)
    sib_add(1)
    down(2)
    gate(3)
    y_mid(1)
    sib_add(2)
    hid_forward(3)
    y_fin(1)
    y_mid(2)
    down(3)
    y_fin(2)
    sib_add(3)
    y_mid(3)
    y_fin(3)
    finish()
    for c in started:
        c.wait_send()


def feed_forward(nrm, w_gate, w_up, w_down):
    depth, width = w_gate.shape
    cols = w_down.shape[1]
    hid_tiles = width // 128
    dn = 512
    down_tiles = cols // dn
    b16 = functools.partial(pltpu.VMEM, dtype=BF16)
    return pl.pallas_call(
        ffn_kernel,
        out_shape=jax.ShapeDtypeStruct((4, 4, cols), BF16),
        in_specs=[pl.BlockSpec(memory_space=pltpu.VMEM)] + [pl.BlockSpec(memory_space=pl.ANY)] * 3,
        out_specs=pl.BlockSpec(memory_space=pltpu.VMEM),
        scratch_shapes=[
            b16((hid_tiles, depth, 256)),
            b16((down_tiles, width, dn)),
            b16((4, 4, depth)),
            pltpu.VMEM((16, depth), F32),
            b16((4, 2, 4, 16, depth)),
            b16((4, 4, 2, 16, 2 * width)),
            b16((4, 16, 2 * width)),
            b16((4, 16, 2 * width)),
            b16((4, 2, 16, 2 * width)),
            b16((4, 2, 16, 2 * width)),
            b16((4, 4, 2, 16, width)),
            b16((4, 2, 4, 16, cols)),
            b16((4, 4, 16, cols)),
            b16((4, 16, cols // 2)),
            b16((4, 16, cols // 2)),
            b16((4, 16, cols)),
            b16((4, 16, cols)),
            b16((4, 16, cols)),
            b16((4, 16, cols)),
            b16((4, 4, cols)),
            b16((4, 4, cols)),
            pltpu.SemaphoreType.DMA((hid_tiles + down_tiles, 2)),
            pltpu.SemaphoreType.DMA((2,)),
            pltpu.SemaphoreType.DMA((COPIES,)),
            pltpu.SemaphoreType.DMA((COPIES,)),
        ],
        compiler_params=pltpu.CompilerParams(
            collective_id=0, has_side_effects=True, vmem_limit_bytes=58 * 1024 * 1024),
        name="ffn",
    )(nrm, w_gate, w_up, w_down)


def body(
    resid,
    queries,
    key_cache,
    value_cache,
    new_keys,
    new_values,
    lengths,
    norm_gain,
    w_gate,
    w_up,
    w_down,
):
    attended = attend(queries, key_cache, value_cache, new_keys, new_values, lengths)
    mixed = resid.astype(jnp.float32) + attended
    mean_square = jnp.mean(mixed * mixed, axis=-1, keepdims=True)
    normed = (mixed * lax.rsqrt(mean_square + 1e-05) * norm_gain.astype(jnp.float32)).astype(
        jnp.bfloat16
    )
    rows, cols = normed.shape
    nrm = normed.reshape(rows, 4, cols // 4).transpose(1, 0, 2)
    ffn = feed_forward(nrm, w_gate, w_up, w_down)
    ffn_out = ffn.transpose(1, 0, 2).reshape(rows, cols)
    return (mixed + ffn_out.astype(jnp.float32)).astype(jnp.bfloat16)


def solution(mesh):
    return jax.shard_map(
        body,
        mesh=mesh,
        in_specs=(
            P(("wide", "narrow"), None),
            P(("wide", "narrow"), None),
            P(("wide", "narrow"), None, None),
            P(("wide", "narrow"), None, None),
            P(("wide", "narrow"), None),
            P(("wide", "narrow"), None),
            P(("wide", "narrow")),
            P(),
            P("narrow", "wide"),
            P("narrow", "wide"),
            P("wide", "narrow"),
        ),
        out_specs=P(("wide", "narrow"), None),
        check_vma=False,
    )
```

```python
import functools

import jax
import jax.numpy as jnp
from jax import lax
from jax.experimental import pallas as pl
from jax.experimental.pallas import tpu as pltpu
from jax.sharding import PartitionSpec as P

HEADS = 128
KVH = 8
HD = 128
MESH = pl.DeviceIdType.MESH
F32 = jnp.float32
BF16 = jnp.bfloat16
COPIES = 112
ORDER = (
    "own", "z0", "yfp", "yfm", "zp", "zm", "z2", "G0",
    "U0", "zfmm", "rA0", "zfpp", "rB0", "S1", "zfp2", "S2",
    "zfm0", "gate0", "G1", "U1", "G2", "S3", "U2", "D0",
    "rA1", "rB1", "G3", "A0", "U3", "V0", "gate1", "rA2",
    "B0", "rA3", "rB2", "rB3", "D1", "V1", "gate2", "A1",
    "yA0", "B1", "gate3", "yA1", "yB0", "D2", "yB1", "V2",
    "A2", "D3", "B2", "V3", "yF1", "A3", "B3", "yA2",
    "yF0", "yB2", "yA3", "yB3", "yF2", "yF3", "end",
)


def attend(query_rows, key_rows, value_rows, key_new, value_new, length_rows):
    count = query_rows.shape[0]
    cached = key_rows.shape[1]
    groups = HEADS // KVH
    qh = query_rows.reshape(count, KVH, groups, HD)
    kh = key_rows.reshape(count, cached, KVH, HD)
    vh = value_rows.reshape(count, cached, KVH, HD)
    kn = key_new.reshape(count, KVH, HD)
    vn = value_new.reshape(count, KVH, HD)
    score_scale = 1.0 / HD**0.5
    scores = jnp.einsum("bgqd,btgd->bgqt", qh, kh, preferred_element_type=jnp.float32) * score_scale
    own = jnp.einsum("bgqd,bgd->bgq", qh, kn, preferred_element_type=jnp.float32) * score_scale
    live = jnp.arange(cached, dtype=jnp.int32)[None, :] < length_rows[:, None]
    live = live[:, None, None, :]
    scores = jnp.where(live, scores, jnp.float32(-1e30))
    row_top = jnp.maximum(jnp.max(scores, axis=-1), own)
    cache_exp = jnp.where(live, jnp.exp(scores - row_top[..., None]), jnp.float32(0.0))
    own_exp = jnp.exp(own - row_top)
    total = jnp.sum(cache_exp, axis=-1) + own_exp
    probs = (cache_exp / total[..., None]).astype(jnp.bfloat16)
    own_prob = (own_exp / total).astype(jnp.bfloat16)
    attended = jnp.einsum("bgqt,btgd->bgqd", probs, vh, preferred_element_type=jnp.float32)
    attended = (
        attended + own_prob.astype(jnp.float32)[..., None] * vn.astype(jnp.float32)[:, :, None, :]
    )
    return attended.reshape(count, HEADS * HD)


def ffn_kernel(
    nrm, wg_hbm, wu_hbm, wd_hbm,
    out,
    wgu, wd, abuf, stage, x_all,
    part, ra, rb, rm, rp, hid,
    dpart, sib, ya, yb, ym, yp, zs, zr,
    wsem, osem, ss, rs,
):
    x = lax.axis_index("narrow")
    w = lax.axis_index("wide")
    z = lax.div(w, 8)
    y = lax.rem(lax.div(w, 2), 4)
    core = lax.rem(w, 2)
    other = 1 - core

    def wrap(v):
        return lax.rem(v + 4, 4)

    def X(d):
        return {"narrow": wrap(x + d)}

    def Y(d):
        return {"wide": z * 8 + wrap(y + d) * 2 + core}

    def Z(d):
        return {"wide": wrap(z + d) * 8 + y * 2 + core}

    def XZ(dx, dz):
        if dz == 0:
            return X(dx)
        if dx == 0:
            return Z(dz)
        return {"narrow": wrap(x + dx), "wide": wrap(z + dz) * 8 + y * 2 + core}

    S = {"wide": w + 1 - 2 * core}
    xp1, xm1, xp2 = wrap(x + 1), wrap(x - 1), wrap(x + 2)
    yp1, ym1, yp2 = wrap(y + 1), wrap(y - 1), wrap(y + 2)
    deltas = (0, 1, -1, 2)

    count = [0]
    started = []
    cp = {}

    def rc(src, dst, dev):
        i = count[0]
        count[0] += 1
        c = pltpu.make_async_remote_copy(
            src_ref=src, dst_ref=dst, send_sem=ss.at[i], recv_sem=rs.at[i],
            device_id=dev, device_id_type=MESH)
        started.append(c)
        c.start()
        return c

    def send(name, src, dst, dev):
        cp[name] = rc(src, dst, dev)

    arrived = set()

    def got(*names):
        for n in names:
            if n not in arrived:
                arrived.add(n)
                cp[n].wait_recv()

    down_tiles = wd.shape[0]
    dn = wd.shape[2]
    width = wgu.shape[2]
    loads = [
        pltpu.make_async_copy(wg_hbm, wgu.at[0], wsem.at[0]),
        pltpu.make_async_copy(wu_hbm, wgu.at[1], wsem.at[1]),
    ]
    dloads = []
    for n in range(down_tiles):
        dloads.append(pltpu.make_async_copy(
            wd_hbm.at[:, pl.ds(n * dn, dn)], wd.at[n], wsem.at[2 + n]))
    for c in loads:
        c.start()
    for c in dloads:
        c.start()

    barrier = pltpu.get_barrier_semaphore()
    peers = [XZ(dx, dz) for dx in range(4) for dz in range(4) if (dx, dz) != (0, 0)]
    peers += [Y(1), Y(3), S]
    for p in peers:
        pl.semaphore_signal(barrier, inc=1, device_id=p, device_id_type=MESH)
    pl.semaphore_wait(barrier, len(peers))

    a2a = [rc(nrm.at[wrap(x + d)], abuf.at[x], X(d)) for d in (1, 2, 3)]
    keep = pltpu.make_async_copy(nrm.at[x], abuf.at[x], osem.at[0])
    keep.start()
    keep.wait()
    for c in a2a:
        c.wait_recv()
    for q in range(4):
        stage[pl.ds(4 * q, 4), :] = abuf[q].astype(F32)
    x_all[z, core, y] = stage[...].astype(BF16)

    half = x_all.shape[4] // 2
    lo = pl.ds(0, half)
    hi = pl.ds(half, half)

    def block(dz, dy):
        return x_all.at[wrap(z + dz), core, wrap(y + dy)]

    ops = {}

    def own():
        b = block(0, 0)
        send("y+a", b.at[:, lo], b.at[:, lo], Y(1))
        send("y-a", b.at[:, hi], b.at[:, hi], Y(-1))
        send("y+b", b.at[:, hi], b.at[:, hi], Y(1))
        send("y-b", b.at[:, lo], b.at[:, lo], Y(-1))
        send("s0", b, b, S)

    ops["own"] = own

    def over_z(r, tag):
        b = block(0, r)
        send("z+" + tag, b, b, Z(1))
        send("z-" + tag, b, b, Z(-1))
        if r:
            send("s" + tag, b, b, S)

    ops["z0"] = lambda: over_z(0, "0")

    def yfm():
        got("y+a")
        b = block(0, -1).at[:, lo]
        send("yf+", b, b, Y(1))

    def yfp():
        got("y-a")
        b = block(0, 1).at[:, hi]
        send("yf-", b, b, Y(-1))

    def zm():
        got("y+b")
        over_z(-1, "m")

    def zp():
        got("y-b")
        over_z(1, "p")

    def z2():
        got("yf+", "yf-")
        over_z(2, "2")

    ops.update(yfm=yfm, yfp=yfp, zm=zm, zp=zp, z2=z2)

    def zf(sign, r, tag):
        d = "+" if sign > 0 else "-"
        got("z" + d + tag)
        b = block(-sign, r)
        send("zf" + d + tag, b, b, Z(sign))

    ops["zfm0"] = lambda: zf(1, 0, "0")
    ops["zfmm"] = lambda: zf(1, -1, "m")
    ops["zfpp"] = lambda: zf(-1, 1, "p")
    ops["zfp2"] = lambda: zf(-1, 2, "2")

    def slab(k, *names):
        got(*names)
        b = x_all.at[wrap(z + deltas[k]), core]
        send("sl%d" % k, b, b, S)

    ops["S1"] = lambda: slab(1, "z-0", "z-m", "z-p", "z-2")
    ops["S2"] = lambda: slab(2, "z+0", "z+m", "z+p", "z+2")
    ops["S3"] = lambda: slab(3, "zf+0", "zf+m", "zf-p", "zf-2")

    def gate_half(k):
        if k == 0:
            for c in loads:
                c.wait()
            got("s0", "sm", "sp", "s2")
        else:
            got("sl%d" % k)
        lhs = x_all[wrap(z + deltas[k])].reshape(128, x_all.shape[4])
        r = jnp.dot(lhs, wgu[0], preferred_element_type=F32).astype(BF16)
        part[k, 0] = r.reshape(4, 32, width)
        send("a%d" % k, part.at[k, 0, xp2], ra.at[k], X(1))
        send("d%d" % k, part.at[k, 0, xm1], rp.at[k, 0], X(-1))

    def up_half(k):
        lhs = x_all[wrap(z + deltas[k])].reshape(128, x_all.shape[4])
        r = jnp.dot(lhs, wgu[1], preferred_element_type=F32).astype(BF16)
        part[k, 1] = r.reshape(4, 32, width)
        send("b%d" % k, part.at[k, 1, xp2], rb.at[k], X(-1))
        send("c%d" % k, part.at[k, 1, xp1], rm.at[k, 1], X(1))

    def mid_a(k):
        got("a%d" % k)
        part[k, 0, xp1] = (part[k, 0, xp1].astype(F32) + ra[k].astype(F32)).astype(BF16)
        send("e%d" % k, part.at[k, 0, xp1], rm.at[k, 0], X(1))

    def mid_b(k):
        got("b%d" % k)
        part[k, 1, xm1] = (part[k, 1, xm1].astype(F32) + rb[k].astype(F32)).astype(BF16)
        send("f%d" % k, part.at[k, 1, xm1], rp.at[k, 1], X(-1))

    def gate(k):
        got("d%d" % k, "c%d" % k, "e%d" % k, "f%d" % k)
        for j in range(width // 128):
            cols = pl.ds(j * 128, 128)

            def total(h):
                return (part[k, h, x, :, cols].astype(F32) + rm[k, h, :, cols].astype(F32)
                        + rp[k, h, :, cols].astype(F32))

            hid[k, x, :, cols] = (jax.nn.silu(total(0)) * total(1)).astype(BF16)
        b = hid.at[k, x]
        send("h+%d" % k, b, b, X(1))
        send("h-%d" % k, b, b, X(-1))
        send("h2%d" % k, b, b, X(2))

    def down(k, h):
        if h == 0:
            if k == 0:
                for c in dloads:
                    c.wait()
            got("h+%d" % k, "h-%d" % k, "h2%d" % k)
        tiles = down_tiles // 2

        def step(n, carry):
            lhs = hid[k].reshape(128, width)
            r = jnp.dot(lhs, wd[h * tiles + n], preferred_element_type=F32).astype(BF16)
            at = pl.multiple_of(h * half + n * dn, dn)
            dpart[k, :, :, :, pl.ds(at, dn)] = r.reshape(2, 4, 16, dn)
            return carry

        lax.fori_loop(0, tiles, step, 0)
        cols = hi if h else lo
        send("EW"[h] + str(k), dpart.at[k, other, :, :, cols], sib.at[k, :, :, cols], S)

    def sib_add(k, h):
        got("EW"[h] + str(k))
        cols = hi if h else lo

        def step(i, carry):
            yi = lax.rem(yp2 + i, 4)
            dpart[k, core, yi, :, cols] = (
                dpart[k, core, yi, :, cols].astype(F32) + sib[k, yi, :, cols].astype(F32)).astype(BF16)
            return carry

        lax.fori_loop(0, 4, step, 0)
        if h == 0:
            send("t1%d" % k, dpart.at[k, core, yp2, :, lo], ya.at[k], Y(1))
            send("t4%d" % k, dpart.at[k, core, ym1, :, lo], yp.at[k, :, lo], Y(-1))
        else:
            send("t2%d" % k, dpart.at[k, core, yp2, :, hi], yb.at[k], Y(-1))
            send("t3%d" % k, dpart.at[k, core, yp1, :, hi], ym.at[k, :, hi], Y(1))

    def y_mid(k, h):
        if h == 0:
            got("t1%d" % k)
            dpart[k, core, yp1, :, lo] = (
                dpart[k, core, yp1, :, lo].astype(F32) + ya[k].astype(F32)).astype(BF16)
            send("t5%d" % k, dpart.at[k, core, yp1, :, lo], ym.at[k, :, lo], Y(1))
        else:
            got("t2%d" % k)
            dpart[k, core, ym1, :, hi] = (
                dpart[k, core, ym1, :, hi].astype(F32) + yb[k].astype(F32)).astype(BF16)
            send("t6%d" % k, dpart.at[k, core, ym1, :, hi], yp.at[k, :, hi], Y(-1))

    def y_fin(k):
        got("t3%d" % k, "t4%d" % k, "t5%d" % k, "t6%d" % k)
        stage[...] = dpart[k, core, y].astype(F32) + ym[k].astype(F32) + yp[k].astype(F32)
        for q in range(4):
            zs[k, q] = stage[pl.ds(4 * q, 4), :].astype(BF16)
        for dx in (2, 1, 3, 0):
            if dx == 0 and k == 0:
                keep = pltpu.make_async_copy(zs.at[k, x], zr.at[k, x], osem.at[1])
                keep.start()
                keep.wait()
            else:
                send("v%d%d" % (k, dx), zs.at[k, wrap(x + dx)], zr.at[k, x], XZ(dx, deltas[k]))

    def finish():
        for k in range(4):
            for dx in range(4):
                if (k, dx) != (0, 0):
                    got("v%d%d" % (k, dx))
        for q in range(4):
            out[q] = (zr[0, q].astype(F32) + zr[1, q].astype(F32) + zr[2, q].astype(F32)
                      + zr[3, q].astype(F32)).astype(BF16)

    for k in range(4):
        n = str(k)
        ops["G" + n] = functools.partial(gate_half, k)
        ops["U" + n] = functools.partial(up_half, k)
        ops["rA" + n] = functools.partial(mid_a, k)
        ops["rB" + n] = functools.partial(mid_b, k)
        ops["gate" + n] = functools.partial(gate, k)
        ops["D" + n] = functools.partial(down, k, 0)
        ops["V" + n] = functools.partial(down, k, 1)
        ops["A" + n] = functools.partial(sib_add, k, 0)
        ops["B" + n] = functools.partial(sib_add, k, 1)
        ops["yA" + n] = functools.partial(y_mid, k, 0)
        ops["yB" + n] = functools.partial(y_mid, k, 1)
        ops["yF" + n] = functools.partial(y_fin, k)
    ops["end"] = finish

    for name in ORDER:
        ops[name]()
    for c in started:
        c.wait_send()


def feed_forward(nrm, w_gate, w_up, w_down):
    depth, width = w_gate.shape
    cols = w_down.shape[1]
    dn = 1024
    down_tiles = cols // dn
    b16 = functools.partial(pltpu.VMEM, dtype=BF16)
    return pl.pallas_call(
        ffn_kernel,
        out_shape=jax.ShapeDtypeStruct((4, 4, cols), BF16),
        in_specs=[pl.BlockSpec(memory_space=pltpu.VMEM)] + [pl.BlockSpec(memory_space=pl.ANY)] * 3,
        out_specs=pl.BlockSpec(memory_space=pltpu.VMEM),
        scratch_shapes=[
            b16((2, depth, width)),
            b16((down_tiles, width, dn)),
            b16((4, 4, depth)),
            pltpu.VMEM((16, depth), F32),
            b16((4, 2, 4, 16, depth)),
            b16((4, 2, 4, 32, width)),
            b16((4, 32, width)),
            b16((4, 32, width)),
            b16((4, 2, 32, width)),
            b16((4, 2, 32, width)),
            b16((4, 4, 32, width)),
            b16((4, 2, 4, 16, cols)),
            b16((4, 4, 16, cols)),
            b16((4, 16, cols // 2)),
            b16((4, 16, cols // 2)),
            b16((4, 16, cols)),
            b16((4, 16, cols)),
            b16((4, 4, 4, cols)),
            b16((4, 4, 4, cols)),
            pltpu.SemaphoreType.DMA((2 + down_tiles,)),
            pltpu.SemaphoreType.DMA((2,)),
            pltpu.SemaphoreType.DMA((COPIES,)),
            pltpu.SemaphoreType.DMA((COPIES,)),
        ],
        compiler_params=pltpu.CompilerParams(
            collective_id=0, has_side_effects=True, vmem_limit_bytes=58 * 1024 * 1024),
        name="ffn",
    )(nrm, w_gate, w_up, w_down)


def body(
    resid,
    queries,
    key_cache,
    value_cache,
    new_keys,
    new_values,
    lengths,
    norm_gain,
    w_gate,
    w_up,
    w_down,
):
    attended = attend(queries, key_cache, value_cache, new_keys, new_values, lengths)
    mixed = resid.astype(jnp.float32) + attended
    mean_square = jnp.mean(mixed * mixed, axis=-1, keepdims=True)
    normed = (mixed * lax.rsqrt(mean_square + 1e-05) * norm_gain.astype(jnp.float32)).astype(
        jnp.bfloat16
    )
    rows, cols = normed.shape
    nrm = normed.reshape(rows, 4, cols // 4).transpose(1, 0, 2)
    ffn = feed_forward(nrm, w_gate, w_up, w_down)
    ffn_out = ffn.transpose(1, 0, 2).reshape(rows, cols)
    return (mixed + ffn_out.astype(jnp.float32)).astype(jnp.bfloat16)


def solution(mesh):
    return jax.shard_map(
        body,
        mesh=mesh,
        in_specs=(
            P(("wide", "narrow"), None),
            P(("wide", "narrow"), None),
            P(("wide", "narrow"), None, None),
            P(("wide", "narrow"), None, None),
            P(("wide", "narrow"), None),
            P(("wide", "narrow"), None),
            P(("wide", "narrow")),
            P(),
            P("narrow", "wide"),
            P("narrow", "wide"),
            P("wide", "narrow"),
        ),
        out_specs=P(("wide", "narrow"), None),
        check_vma=False,
    )
```

```python
import functools

import jax
import jax.numpy as jnp
from jax import lax
from jax.experimental import pallas as pl
from jax.experimental.pallas import tpu as pltpu
from jax.sharding import PartitionSpec as P

HEADS = 128
KVH = 8
HD = 128
MESH = pl.DeviceIdType.MESH
F32 = jnp.float32
BF16 = jnp.bfloat16
COPIES = 140
ORDER = (
    "own", "z0", "yfm", "yfp", "zfm0", "zm", "yq1", "zp",
    "yq2", "z2", "G0", "U0", "zfp2", "yq3", "zfmm", "S1",
    "S2", "zfpp", "rA0", "rB0", "G1", "U1", "G2", "U2",
    "S3", "gate0", "rA1", "rB1", "G3", "U3", "D0", "rB2",
    "rA2", "V0", "gate1", "rA3", "B0", "A0", "rB3", "gate2",
    "D1", "V1", "yA0", "yB0", "gate3", "A1", "D2", "B1",
    "V2", "A2", "D3", "B2", "yB1", "yA1", "V3", "A3",
    "yA2", "B3", "yB2", "yH0", "yH1", "yA3", "yL2", "yL0",
    "yL1", "yB3", "yH2", "yL3", "yH3", "end",
)


def scaled_scores(q, k):
    return lax.dot_general(q, k, (((1,), (1,)), ((), ())), preferred_element_type=F32) * (1.0 / HD**0.5)


def layer_kernel(
    lens_hbm, nk_hbm, nv_hbm, gain_hbm, q_hbm, resid_hbm, k_hbm, v_hbm, wg_hbm, wu_hbm, wd_hbm,
    out,
    lens, nk, nv, gain, q, resid, kc, vc, nkv, bias, mixed, wide32, nrm,
    wgu, wd, abuf, stage, x_all,
    part, ra, rb, rm, rp, hid,
    dpart, sib, ya, yb, ym, yp, zs, zr,
    isem, wsem, osem, ss, rs,
):
    x = lax.axis_index("narrow")
    w = lax.axis_index("wide")
    z = lax.div(w, 8)
    y = lax.rem(lax.div(w, 2), 4)
    core = lax.rem(w, 2)
    other = 1 - core

    def wrap(v):
        return lax.rem(v + 4, 4)

    def X(d):
        return {"narrow": wrap(x + d)}

    def Y(d):
        return {"wide": z * 8 + wrap(y + d) * 2 + core}

    def Z(d):
        return {"wide": wrap(z + d) * 8 + y * 2 + core}

    def XZ(dx, dz):
        if dz == 0:
            return X(dx)
        if dx == 0:
            return Z(dz)
        return {"narrow": wrap(x + dx), "wide": wrap(z + dz) * 8 + y * 2 + core}

    S = {"wide": w + 1 - 2 * core}
    xp1, xm1, xp2 = wrap(x + 1), wrap(x - 1), wrap(x + 2)
    yp1, ym1, yp2 = wrap(y + 1), wrap(y - 1), wrap(y + 2)
    deltas = (0, 1, -1, 2)

    count = [0]
    started = []
    cp = {}

    def rc(src, dst, dev):
        i = count[0]
        count[0] += 1
        c = pltpu.make_async_remote_copy(
            src_ref=src, dst_ref=dst, send_sem=ss.at[i], recv_sem=rs.at[i],
            device_id=dev, device_id_type=MESH)
        started.append(c)
        c.start()
        return c

    def send(name, src, dst, dev):
        cp[name] = rc(src, dst, dev)

    arrived = set()

    def got(*names):
        for n in names:
            if n not in arrived:
                arrived.add(n)
                cp[n].wait_recv()

    seqs, cached = kc.shape[0], kc.shape[1]
    early = [pltpu.make_async_copy(q_hbm, q, isem.at[0, 0])]
    early += [pltpu.make_async_copy(k_hbm.at[b], kc.at[b], isem.at[1, b]) for b in range(seqs)]
    early += [pltpu.make_async_copy(v_hbm.at[b], vc.at[b], isem.at[2, b]) for b in range(seqs)]
    small = [
        pltpu.make_async_copy(lens_hbm, lens, isem.at[3, 0]),
        pltpu.make_async_copy(nk_hbm, nk, isem.at[3, 1]),
        pltpu.make_async_copy(nv_hbm, nv, isem.at[3, 2]),
        pltpu.make_async_copy(gain_hbm, gain, isem.at[3, 3]),
    ]
    late = pltpu.make_async_copy(resid_hbm, resid, isem.at[0, 1])
    early.append(late)
    for c in small + early:
        c.start()

    barrier = pltpu.get_barrier_semaphore()
    peers = [XZ(dx, dz) for dx in range(4) for dz in range(4) if (dx, dz) != (0, 0)]
    peers += [Y(1), Y(2), Y(3), S]
    for p in peers:
        pl.semaphore_signal(barrier, inc=1, device_id=p, device_id_type=MESH)

    group_rows = q.shape[0] // KVH
    shape = (group_rows, seqs * cached)
    row_seq = lax.broadcasted_iota(jnp.int32, shape, 0) & 3
    col = lax.broadcasted_iota(jnp.int32, shape, 1)
    col_seq = jnp.zeros(shape, jnp.int32)
    for b in range(1, seqs):
        col_seq = col_seq + (col >= b * cached).astype(jnp.int32)
    rows_all = q.shape[0]
    pick = ((lax.broadcasted_iota(jnp.int32, (rows_all, HEADS), 0) >> 2)
            == lax.broadcasted_iota(jnp.int32, (rows_all, HEADS), 1))
    pick = jnp.where(pick, F32(1.0), F32(0.0)).astype(BF16)
    own_seq = (lax.broadcasted_iota(jnp.int32, (group_rows, 16), 0) & 3) == lax.broadcasted_iota(
        jnp.int32, (group_rows, 16), 1)
    stage[...] = jnp.zeros_like(stage)
    for c in small:
        c.wait()
    limit = jnp.zeros(shape, jnp.int32)
    for b in range(seqs):
        limit = jnp.where(row_seq == b, lens[b] + b * cached, limit)
    bias[...] = jnp.where((col_seq == row_seq) & (col < limit), F32(0.0), F32(-1e30))
    width_kv = nk.shape[1]
    stage[pl.ds(0, 4), pl.ds(0, width_kv)] = nk[...].astype(F32)
    stage[pl.ds(0, 4), pl.ds(width_kv, width_kv)] = nv[...].astype(F32)
    nkv[...] = stage[:, pl.ds(0, 2 * width_kv)].astype(BF16)
    wide32[...] = jnp.dot(pick, gain[...], preferred_element_type=F32)

    for c in early:
        c.wait()

    down_tiles = wd.shape[0]
    dn = wd.shape[2]
    width = wgu.shape[2]
    loads = [
        pltpu.make_async_copy(wg_hbm, wgu.at[0], wsem.at[0]),
        pltpu.make_async_copy(wu_hbm, wgu.at[1], wsem.at[1]),
    ]
    dloads = []
    for n in range(down_tiles):
        dloads.append(pltpu.make_async_copy(
            wd_hbm.at[:, pl.ds(n * dn, dn)], wd.at[n], wsem.at[2 + n]))
    for c in loads:
        c.start()
    for c in dloads:
        c.start()

    def attend(g, carry):
        rows = pl.ds(pl.multiple_of(g * group_rows, group_rows), group_rows)
        lanes = pl.ds(pl.multiple_of(g * HD, HD), HD)
        vlanes = pl.ds(pl.multiple_of(width_kv + g * HD, HD), HD)
        qg = q[rows, :]
        scores = scaled_scores(qg, kc[:, :, lanes].reshape(seqs * cached, HD)) + bias[...]
        own = scaled_scores(qg, nkv[:, lanes])
        own = jnp.sum(jnp.where(own_seq, own, F32(0.0)), axis=1, keepdims=True)
        top = jnp.maximum(jnp.max(scores, axis=1, keepdims=True), own)
        cache_exp = jnp.exp(scores - top)
        own_exp = jnp.exp(own - top)
        inverse = 1.0 / (jnp.sum(cache_exp, axis=1, keepdims=True) + own_exp)
        probs = (cache_exp * inverse).astype(BF16)
        own_prob = jnp.where(own_seq, own_exp * inverse, F32(0.0)).astype(BF16)
        attended = jnp.dot(probs, vc[:, :, lanes].reshape(seqs * cached, HD), preferred_element_type=F32)
        attended = attended + jnp.dot(own_prob, nkv[:, vlanes], preferred_element_type=F32)
        m = resid[rows, :].astype(F32) + attended
        mixed[rows, :] = m
        return carry + jnp.sum((m * m).reshape(group_rows // 8, 8, HD), axis=0)

    squares = lax.fori_loop(0, KVH, attend, jnp.zeros((8, HD), F32), unroll=True)
    squares = jnp.broadcast_to(jnp.sum(squares, axis=1, keepdims=True), (8, HD))
    squares = squares + pltpu.roll(squares, 4, 0)
    inv_rms = lax.rsqrt(squares * (1.0 / (HEADS * HD)) + 1e-05)
    scale8 = jnp.broadcast_to(inv_rms[None], (rows_all // 8, 8, HD))
    normed = mixed[...].reshape(rows_all // 8, 8, HD) * scale8 * wide32[...].reshape(rows_all // 8, 8, HD)
    nrm[...] = normed.reshape(rows_all, HD).astype(BF16).reshape(nrm.shape)

    pl.semaphore_wait(barrier, len(peers))
    a2a = [rc(nrm.at[wrap(x + d)], abuf.at[x], X(d)) for d in (2, 1, 3)]
    keep = pltpu.make_async_copy(nrm.at[x], abuf.at[x], osem.at[0])
    keep.start()
    keep.wait()
    for c in a2a:
        c.wait_recv()
    block_rows = abuf.shape[1]
    block_heads = block_rows // seqs
    for n in range(4):
        wide32[pl.ds(n * block_rows, block_rows), :] = abuf[n].astype(F32)
    for n in range(4):
        for h in range(block_heads):
            stage[pl.ds(4 * n, 4), pl.ds(h * HD, HD)] = wide32[pl.ds(n * block_rows + 4 * h, 4), :]
    x_all[z, core, y] = stage[...].astype(BF16)

    half = x_all.shape[4] // 2
    lo = pl.ds(0, half)
    hi = pl.ds(half, half)

    def block(dz, dy):
        return x_all.at[wrap(z + dz), core, wrap(y + dy)]

    ops = {}

    def own():
        b = block(0, 0)
        send("y+a", b.at[:, lo], b.at[:, lo], Y(1))
        send("y-a", b.at[:, hi], b.at[:, hi], Y(-1))
        send("y+b", b.at[:, hi], b.at[:, hi], Y(1))
        send("y-b", b.at[:, lo], b.at[:, lo], Y(-1))
        send("s0", b, b, S)

    ops["own"] = own

    def over_z(r, tag):
        b = block(0, r)
        if r == 0:
            h = b.at[:, hi]
            send("q+", h, h, Z(1))
            send("q-", h, h, Z(-1))
        send("z+" + tag, b.at[:, lo], b.at[:, lo], Z(1))
        send("z-" + tag, b.at[:, lo], b.at[:, lo], Z(-1))
        if r == 0:
            send("q2", h, h, Z(2))
        else:
            send("s" + tag, b, b, S)

    def over_y(i, dep):
        got(dep)
        b = block(deltas[i], 0).at[:, hi]
        send("u%dm" % i, b, b, Y(1))
        send("u%dp" % i, b, b, Y(-1))
        send("u%d2" % i, b, b, Y(2))

    ops["yq1"] = lambda: over_y(1, "q-")
    ops["yq2"] = lambda: over_y(2, "q+")
    ops["yq3"] = lambda: over_y(3, "q2")

    ops["z0"] = lambda: over_z(0, "0")

    def yfm():
        got("y+a")
        b = block(0, -1).at[:, lo]
        send("yf+", b, b, Y(1))

    def yfp():
        got("y-a")
        b = block(0, 1).at[:, hi]
        send("yf-", b, b, Y(-1))

    def zm():
        got("y+b")
        over_z(-1, "m")

    def zp():
        got("y-b")
        over_z(1, "p")

    def z2():
        got("yf+", "yf-")
        over_z(2, "2")

    ops.update(yfm=yfm, yfp=yfp, zm=zm, zp=zp, z2=z2)

    def zf(sign, r, tag):
        d = "+" if sign > 0 else "-"
        got("z" + d + tag)
        b = block(-sign, r).at[:, lo]
        send("zf" + d + tag, b, b, Z(sign))

    ops["zfm0"] = lambda: zf(1, 0, "0")
    ops["zfmm"] = lambda: zf(1, -1, "m")
    ops["zfpp"] = lambda: zf(-1, 1, "p")
    ops["zfp2"] = lambda: zf(-1, 2, "2")

    def slab(k, *names):
        got(*names)
        got("u%dm" % k, "u%dp" % k, "u%d2" % k)
        b = x_all.at[wrap(z + deltas[k]), core]
        send("sl%d" % k, b, b, S)

    ops["S1"] = lambda: slab(1, "q-", "z-0", "z-m", "z-p", "z-2")
    ops["S2"] = lambda: slab(2, "q+", "z+0", "z+m", "z+p", "z+2")
    ops["S3"] = lambda: slab(3, "q2", "zf+0", "zf+m", "zf-p", "zf-2")

    def gate_half(k):
        if k == 0:
            for c in loads:
                c.wait()
            got("s0", "sm", "sp", "s2")
        else:
            got("sl%d" % k)
        lhs = x_all[wrap(z + deltas[k])].reshape(128, x_all.shape[4])
        r = jnp.dot(lhs, wgu[0], preferred_element_type=F32).astype(BF16)
        part[k, 0] = r.reshape(4, 32, width)
        send("a%d" % k, part.at[k, 0, xp2], ra.at[k], X(1))
        send("d%d" % k, part.at[k, 0, xm1], rp.at[k, 0], X(-1))

    def up_half(k):
        lhs = x_all[wrap(z + deltas[k])].reshape(128, x_all.shape[4])
        r = jnp.dot(lhs, wgu[1], preferred_element_type=F32).astype(BF16)
        part[k, 1] = r.reshape(4, 32, width)
        send("b%d" % k, part.at[k, 1, xp2], rb.at[k], X(-1))
        send("c%d" % k, part.at[k, 1, xp1], rm.at[k, 1], X(1))

    def mid_a(k):
        got("a%d" % k)
        part[k, 0, xp1] = (part[k, 0, xp1].astype(F32) + ra[k].astype(F32)).astype(BF16)
        send("e%d" % k, part.at[k, 0, xp1], rm.at[k, 0], X(1))

    def mid_b(k):
        got("b%d" % k)
        part[k, 1, xm1] = (part[k, 1, xm1].astype(F32) + rb[k].astype(F32)).astype(BF16)
        send("f%d" % k, part.at[k, 1, xm1], rp.at[k, 1], X(-1))

    def gate(k):
        got("d%d" % k, "c%d" % k, "e%d" % k, "f%d" % k)
        for j in range(width // 128):
            cols = pl.ds(j * 128, 128)

            def total(h):
                return (part[k, h, x, :, cols].astype(F32) + rm[k, h, :, cols].astype(F32)
                        + rp[k, h, :, cols].astype(F32))

            hid[k, x, :, cols] = (jax.nn.silu(total(0)) * total(1)).astype(BF16)
        b = hid.at[k, x]
        send("h+%d" % k, b, b, X(1))
        send("h-%d" % k, b, b, X(-1))
        send("h2%d" % k, b, b, X(2))

    def down(k, h):
        if h == 0:
            if k == 0:
                for c in dloads:
                    c.wait()
            got("h+%d" % k, "h-%d" % k, "h2%d" % k)
        tiles = down_tiles // 2

        def step(n, carry):
            lhs = hid[k].reshape(128, width)
            r = jnp.dot(lhs, wd[h * tiles + n], preferred_element_type=F32).astype(BF16)
            at = pl.multiple_of(h * half + n * dn, dn)
            dpart[k, :, :, :, pl.ds(at, dn)] = r.reshape(2, 4, 16, dn)
            return carry

        lax.fori_loop(0, tiles, step, 0)
        cols = hi if h else lo
        send("EW"[h] + str(k), dpart.at[k, other, :, :, cols], sib.at[k, :, :, cols], S)

    def sib_add(k, h):
        got("EW"[h] + str(k))
        cols = hi if h else lo

        def step(i, carry):
            yi = lax.rem(yp2 + i, 4)
            dpart[k, core, yi, :, cols] = (
                dpart[k, core, yi, :, cols].astype(F32) + sib[k, yi, :, cols].astype(F32)).astype(BF16)
            return carry

        lax.fori_loop(0, 4, step, 0)
        if h == 0:
            send("t1%d" % k, dpart.at[k, core, yp2, :, lo], ya.at[k], Y(1))
            send("t4%d" % k, dpart.at[k, core, ym1, :, lo], yp.at[k, :, lo], Y(-1))
        else:
            send("t2%d" % k, dpart.at[k, core, yp2, :, hi], yb.at[k], Y(-1))
            send("t3%d" % k, dpart.at[k, core, yp1, :, hi], ym.at[k, :, hi], Y(1))

    def y_mid(k, h):
        if h == 0:
            got("t1%d" % k)
            dpart[k, core, yp1, :, lo] = (
                dpart[k, core, yp1, :, lo].astype(F32) + ya[k].astype(F32)).astype(BF16)
            send("t5%d" % k, dpart.at[k, core, yp1, :, lo], ym.at[k, :, lo], Y(1))
        else:
            got("t2%d" % k)
            dpart[k, core, ym1, :, hi] = (
                dpart[k, core, ym1, :, hi].astype(F32) + yb[k].astype(F32)).astype(BF16)
            send("t6%d" % k, dpart.at[k, core, ym1, :, hi], yp.at[k, :, hi], Y(-1))

    def y_fin(k, h):
        cols = hi if h else lo
        if h == 0:
            got("t4%d" % k, "t5%d" % k)
        else:
            got("t3%d" % k, "t6%d" % k)
        stage[:, cols] = (dpart[k, core, y, :, cols].astype(F32) + ym[k, :, cols].astype(F32)
                          + yp[k, :, cols].astype(F32))
        part_rows = block_rows // 2
        first = h * part_rows
        piece = pl.ds(first, part_rows)
        for n in range(4):
            for i in range(block_heads // 2):
                head = h * (block_heads // 2) + i
                wide32[pl.ds(n * block_rows + 4 * head, 4), :] = stage[pl.ds(4 * n, 4), pl.ds(head * HD, HD)]
            zs[k, n, piece, :] = wide32[pl.ds(n * block_rows + first, part_rows), :].astype(BF16)
        for dx in (2, 1, 3, 0):
            if dx == 0 and k == 0:
                keep = pltpu.make_async_copy(zs.at[k, x, piece], zr.at[k, x, piece], osem.at[1 + h])
                keep.start()
                keep.wait()
            else:
                send("v%d%d%d" % (k, dx, h), zs.at[k, wrap(x + dx), piece], zr.at[k, x, piece],
                     XZ(dx, deltas[k]))

    def finish():
        for k in range(4):
            for dx in range(4):
                if (k, dx) != (0, 0):
                    got("v%d%d0" % (k, dx), "v%d%d1" % (k, dx))
        for n in range(4):
            ffn = (zr[0, n].astype(F32) + zr[1, n].astype(F32) + zr[2, n].astype(F32)
                   + zr[3, n].astype(F32)).astype(BF16)
            rows = pl.ds(n * block_rows, block_rows)
            out[rows, :] = mixed[rows, :] + ffn.astype(F32)

    for k in range(4):
        n = str(k)
        ops["G" + n] = functools.partial(gate_half, k)
        ops["U" + n] = functools.partial(up_half, k)
        ops["rA" + n] = functools.partial(mid_a, k)
        ops["rB" + n] = functools.partial(mid_b, k)
        ops["gate" + n] = functools.partial(gate, k)
        ops["D" + n] = functools.partial(down, k, 0)
        ops["V" + n] = functools.partial(down, k, 1)
        ops["A" + n] = functools.partial(sib_add, k, 0)
        ops["B" + n] = functools.partial(sib_add, k, 1)
        ops["yA" + n] = functools.partial(y_mid, k, 0)
        ops["yB" + n] = functools.partial(y_mid, k, 1)
        ops["yL" + n] = functools.partial(y_fin, k, 0)
        ops["yH" + n] = functools.partial(y_fin, k, 1)
    ops["end"] = finish

    for name in ORDER:
        ops[name]()
    for c in started:
        c.wait_send()


def by_head(a):
    rows, cols = a.shape
    return a.reshape(rows, HEADS, HD).transpose(1, 0, 2).reshape(rows * HEADS, HD)


def body(
    resid,
    queries,
    key_cache,
    value_cache,
    new_keys,
    new_values,
    lengths,
    norm_gain,
    w_gate,
    w_up,
    w_down,
):
    depth, width = w_gate.shape
    cols = w_down.shape[1]
    seqs, cached, kv = key_cache.shape
    rows = seqs * HEADS
    dn = 1024
    down_tiles = cols // dn
    b16 = functools.partial(pltpu.VMEM, dtype=BF16)
    out = pl.pallas_call(
        layer_kernel,
        out_shape=jax.ShapeDtypeStruct((rows, HD), F32),
        in_specs=[pl.BlockSpec(memory_space=pl.ANY)] * 11,
        out_specs=pl.BlockSpec(memory_space=pltpu.VMEM),
        scratch_shapes=[
            pltpu.SMEM((seqs,), jnp.int32),
            b16((seqs, kv)),
            b16((seqs, kv)),
            b16((HEADS, HD)),
            b16((rows, HD)),
            b16((rows, HD)),
            b16((seqs, cached, kv)),
            b16((seqs, cached, kv)),
            b16((16, 2 * kv)),
            pltpu.VMEM((rows // KVH, seqs * cached), F32),
            pltpu.VMEM((rows, HD), F32),
            pltpu.VMEM((rows, HD), F32),
            b16((4, rows // 4, HD)),
            b16((2, depth, width)),
            b16((down_tiles, width, dn)),
            b16((4, rows // 4, HD)),
            pltpu.VMEM((16, depth), F32),
            b16((4, 2, 4, 16, depth)),
            b16((4, 2, 4, 32, width)),
            b16((4, 32, width)),
            b16((4, 32, width)),
            b16((4, 2, 32, width)),
            b16((4, 2, 32, width)),
            b16((4, 4, 32, width)),
            b16((4, 2, 4, 16, cols)),
            b16((4, 4, 16, cols)),
            b16((4, 16, cols // 2)),
            b16((4, 16, cols // 2)),
            b16((4, 16, cols)),
            b16((4, 16, cols)),
            b16((4, 4, rows // 4, HD)),
            b16((4, 4, rows // 4, HD)),
            pltpu.SemaphoreType.DMA((4, seqs)),
            pltpu.SemaphoreType.DMA((2 + down_tiles,)),
            pltpu.SemaphoreType.DMA((3,)),
            pltpu.SemaphoreType.DMA((COPIES,)),
            pltpu.SemaphoreType.DMA((COPIES,)),
        ],
        compiler_params=pltpu.CompilerParams(
            collective_id=0, has_side_effects=True, vmem_limit_bytes=58 * 1024 * 1024),
        name="layer",
    )(lengths, new_keys, new_values, norm_gain.reshape(HEADS, HD), by_head(queries), by_head(resid),
      key_cache, value_cache, w_gate, w_up, w_down)
    return out.astype(BF16).reshape(HEADS, seqs, HD).transpose(1, 0, 2).reshape(seqs, HEADS * HD)


def solution(mesh):
    return jax.shard_map(
        body,
        mesh=mesh,
        in_specs=(
            P(("wide", "narrow"), None),
            P(("wide", "narrow"), None),
            P(("wide", "narrow"), None, None),
            P(("wide", "narrow"), None, None),
            P(("wide", "narrow"), None),
            P(("wide", "narrow"), None),
            P(("wide", "narrow")),
            P(),
            P("narrow", "wide"),
            P("narrow", "wide"),
            P("wide", "narrow"),
        ),
        out_specs=P(("wide", "narrow"), None),
        check_vma=False,
    )
```

```python
import functools

import jax
import jax.numpy as jnp
from jax import lax
from jax.experimental import pallas as pl
from jax.experimental.pallas import tpu as pltpu
from jax.sharding import PartitionSpec as P

HEADS = 128
KVH = 8
HD = 128
MESH = pl.DeviceIdType.MESH
F32 = jnp.float32
BF16 = jnp.bfloat16
ARRIVALS = 67
DEPARTURES = 15
ORDER = (
    "own", "z0", "yfm", "yfp", "yq1", "yq2", "zm", "zp",
    "z2", "G0", "U0", "zfm0", "zfmm", "zfpp", "zfp2", "yq3",
    "S1", "S2", "rA0", "rB0", "G1", "U1", "G2", "U2",
    "S3", "gate0", "rA1", "rB1", "G3", "U3", "D0", "rB2",
    "rA2", "V0", "gate1", "rA3", "B0", "A0", "rB3", "gate2",
    "D1", "V1", "yA0", "yB0", "gate3", "A1", "D2", "B1",
    "V2", "A2", "D3", "B2", "yB1", "yA1", "V3", "A3",
    "yA2", "B3", "yB2", "yH0", "yH1", "yA3", "yL2", "yL0",
    "yL1", "yB3", "yH2", "yL3", "yH3", "end",
)


def scaled_scores(q, k):
    return lax.dot_general(q, k, (((1,), (1,)), ((), ())), preferred_element_type=F32) * (1.0 / HD**0.5)


def layer_kernel(
    lens_hbm, nk_hbm, nv_hbm, gain_hbm, q_hbm, resid_hbm, k_hbm, v_hbm, wg_hbm, wu_hbm, wd_hbm,
    out,
    lens, nk, nv, gain, q, resid, kc, vc, nkv, bias, mixed, wide32, nrm,
    wgu, wd, abuf, stage, x_all,
    part, ra, rb, rm, rp, hid,
    dpart, sib, ya, yb, ym, yp, zs, zr,
    isem, wsem, osem, ss, rs,
):
    x = lax.axis_index("narrow")
    w = lax.axis_index("wide")
    z = lax.div(w, 8)
    y = lax.rem(lax.div(w, 2), 4)
    core = lax.rem(w, 2)
    other = 1 - core

    def wrap(v):
        return lax.rem(v + 4, 4)

    def X(d):
        return {"narrow": wrap(x + d)}

    def Y(d):
        return {"wide": z * 8 + wrap(y + d) * 2 + core}

    def Z(d):
        return {"wide": wrap(z + d) * 8 + y * 2 + core}

    def XZ(dx, dz):
        if dz == 0:
            return X(dx)
        if dx == 0:
            return Z(dz)
        return {"narrow": wrap(x + dx), "wide": wrap(z + dz) * 8 + y * 2 + core}

    S = {"wide": w + 1 - 2 * core}
    xp1, xm1, xp2 = wrap(x + 1), wrap(x - 1), wrap(x + 2)
    yp1, ym1, yp2 = wrap(y + 1), wrap(y - 1), wrap(y + 2)
    deltas = (0, 1, -1, 2)

    half = x_all.shape[4] // 2
    lo = pl.ds(0, half)
    hi = pl.ds(half, half)
    halves = x_all.at[0, 0, :, :, lo]
    recv_groups = [
        (("s0", "sm", "sp", "s2"), sib.at[0]),
        (("yf+", "yf-"), ym.at[0]),
        (("z-0", "z-m"), ym.at[0]),
        (("z+p", "z+2"), ym.at[0]),
        (("zf+0", "zf+m", "zf-p", "zf-2"), halves),
        (("n1", "n2", "n3"), nrm.at[pl.ds(0, 3)]),
    ]
    send_groups = [
        (("n1", "n2", "n3"), nrm.at[pl.ds(0, 3)]),
        (tuple("h2%d" % k for k in range(4)), hid.at[0]),
        (tuple(t + str(k) for k in range(4) for t in "EW"), sib),
        (tuple("t%d%d" % (t, k) for k in range(4) for t in range(1, 7)), sib.at[pl.ds(0, 3)]),
        (("s0", "sm", "sp", "s2", "sl1", "sl2", "sl3"), sib),
        (("y+a", "y-a", "y+b", "y-b", "yf+", "yf-"), sib.at[0, pl.ds(0, 3)]),
        (("z+0", "z-0", "z+m", "z-m", "z+p", "z-p", "z+2", "z-2", "zf+0", "zf+m", "zf-p", "zf-2", "q+", "q-",
          "q2") + tuple("u%d%s" % (k, t) for k in (1, 2, 3) for t in "mp2"), sib.at[pl.ds(0, 3)]),
    ]
    for k in range(4):
        if k:
            recv_groups.append((tuple("u%d%s" % (k, t) for t in "mp2"), x_all.at[0, 0, pl.ds(0, 3), :, lo]))
        recv_groups.append((tuple(t + str(k) for t in "cdef"), hid.at[k]))
        recv_groups.append((tuple("h%s%d" % (t, k) for t in "+-2"), hid.at[k, pl.ds(0, 3)]))
        recv_groups.append((("t4%d" % k, "t5%d" % k), ym.at[k]))
        recv_groups.append((("t3%d" % k, "t6%d" % k), ym.at[k]))
        send_groups.append((tuple(t + str(k) for t in "abcdef") + ("h+%d" % k, "h-%d" % k), part.at[k]))
        pieces = tuple("v%d%d%d" % (k, dx, h) for dx in range(4) for h in range(2) if k or dx)
        ref = zs.at[k] if k else zs.at[0, pl.ds(0, 3)]
        recv_groups.append((pieces, ref))
        send_groups.append((pieces, ref))
    recv_of = {n: i for i, g in enumerate(recv_groups) for n in g[0]}
    send_of = {n: i for i, g in enumerate(send_groups) for n in g[0]}

    count = [len(recv_groups)]
    started = []
    arrived = set()
    cp = {}

    def send(name, src, dst, dev):
        i = recv_of.get(name)
        if i is None:
            i = count[0]
            count[0] += 1
        c = pltpu.make_async_remote_copy(
            src_ref=src, dst_ref=dst, send_sem=ss.at[send_of[name]], recv_sem=rs.at[i],
            device_id=dev, device_id_type=MESH)
        started.append(name)
        c.start()
        cp[name] = c

    def sum_of(ref, i, j):
        return pltpu.make_async_remote_copy(
            src_ref=ref, dst_ref=ref, send_sem=ss.at[i], recv_sem=rs.at[j], device_id=X(1), device_id_type=MESH)

    def got(*names):
        for n in names:
            if n in arrived:
                continue
            if n in recv_of:
                members, ref = recv_groups[recv_of[n]]
                assert set(members) <= set(names) and set(members) <= set(started)
                sum_of(ref, 0, recv_of[n]).wait_recv()
                arrived.update(members)
            else:
                cp[n].wait_recv()
                arrived.add(n)

    seqs, cached = kc.shape[0], kc.shape[1]
    early = [pltpu.make_async_copy(q_hbm, q, isem.at[0, 0])]
    early += [pltpu.make_async_copy(k_hbm.at[b], kc.at[b], isem.at[1, b]) for b in range(seqs)]
    early += [pltpu.make_async_copy(v_hbm.at[b], vc.at[b], isem.at[2, b]) for b in range(seqs)]
    small = [
        pltpu.make_async_copy(lens_hbm, lens, isem.at[3, 0]),
        pltpu.make_async_copy(nk_hbm, nk, isem.at[3, 1]),
        pltpu.make_async_copy(nv_hbm, nv, isem.at[3, 2]),
        pltpu.make_async_copy(gain_hbm, gain, isem.at[3, 3]),
    ]
    late = pltpu.make_async_copy(resid_hbm, resid, isem.at[0, 1])
    early.append(late)
    for c in small + early:
        c.start()

    barrier = pltpu.get_barrier_semaphore()
    peers = [XZ(dx, dz) for dx in range(4) for dz in range(4) if (dx, dz) != (0, 0)]
    peers += [Y(1), Y(2), Y(3), S]
    for p in peers:
        pl.semaphore_signal(barrier, inc=1, device_id=p, device_id_type=MESH)

    group_rows = q.shape[0] // KVH
    shape = (group_rows, seqs * cached)
    row_seq = lax.broadcasted_iota(jnp.int32, shape, 0) & 3
    col = lax.broadcasted_iota(jnp.int32, shape, 1)
    col_seq = jnp.zeros(shape, jnp.int32)
    for b in range(1, seqs):
        col_seq = col_seq + (col >= b * cached).astype(jnp.int32)
    rows_all = q.shape[0]
    pick = ((lax.broadcasted_iota(jnp.int32, (rows_all, HEADS), 0) >> 2)
            == lax.broadcasted_iota(jnp.int32, (rows_all, HEADS), 1))
    pick = jnp.where(pick, F32(1.0), F32(0.0)).astype(BF16)
    own_seq = (lax.broadcasted_iota(jnp.int32, (group_rows, 16), 0) & 3) == lax.broadcasted_iota(
        jnp.int32, (group_rows, 16), 1)
    stage[...] = jnp.zeros_like(stage)
    for c in small:
        c.wait()
    limit = jnp.zeros(shape, jnp.int32)
    for b in range(seqs):
        limit = jnp.where(row_seq == b, lens[b] + b * cached, limit)
    bias[...] = jnp.where((col_seq == row_seq) & (col < limit), F32(0.0), F32(-1e30))
    width_kv = nk.shape[1]
    stage[pl.ds(0, 4), pl.ds(0, width_kv)] = nk[...].astype(F32)
    stage[pl.ds(0, 4), pl.ds(width_kv, width_kv)] = nv[...].astype(F32)
    nkv[...] = stage[:, pl.ds(0, 2 * width_kv)].astype(BF16)
    wide32[...] = jnp.dot(pick, gain[...], preferred_element_type=F32)

    for c in early:
        c.wait()

    down_tiles = wd.shape[0]
    dn = wd.shape[2]
    width = wgu.shape[2]
    loads = [
        pltpu.make_async_copy(wg_hbm, wgu.at[0], wsem.at[0]),
        pltpu.make_async_copy(wu_hbm, wgu.at[1], wsem.at[1]),
    ]
    dloads = []
    for n in range(down_tiles):
        dloads.append(pltpu.make_async_copy(
            wd_hbm.at[:, pl.ds(n * dn, dn)], wd.at[n], wsem.at[2 + n]))
    for c in loads:
        c.start()
    for c in dloads:
        c.start()

    def attend(g, carry):
        rows = pl.ds(pl.multiple_of(g * group_rows, group_rows), group_rows)
        lanes = pl.ds(pl.multiple_of(g * HD, HD), HD)
        vlanes = pl.ds(pl.multiple_of(width_kv + g * HD, HD), HD)
        qg = q[rows, :]
        scores = scaled_scores(qg, kc[:, :, lanes].reshape(seqs * cached, HD)) + bias[...]
        own = scaled_scores(qg, nkv[:, lanes])
        own = jnp.sum(jnp.where(own_seq, own, F32(0.0)), axis=1, keepdims=True)
        top = jnp.maximum(jnp.max(scores, axis=1, keepdims=True), own)
        cache_exp = jnp.exp(scores - top)
        own_exp = jnp.exp(own - top)
        inverse = 1.0 / (jnp.sum(cache_exp, axis=1, keepdims=True) + own_exp)
        probs = (cache_exp * inverse).astype(BF16)
        own_prob = jnp.where(own_seq, own_exp * inverse, F32(0.0)).astype(BF16)
        attended = jnp.dot(probs, vc[:, :, lanes].reshape(seqs * cached, HD), preferred_element_type=F32)
        attended = attended + jnp.dot(own_prob, nkv[:, vlanes], preferred_element_type=F32)
        m = resid[rows, :].astype(F32) + attended
        mixed[rows, :] = m
        return carry + jnp.sum((m * m).reshape(group_rows // 8, 8, HD), axis=0)

    squares = lax.fori_loop(0, KVH, attend, jnp.zeros((8, HD), F32), unroll=True)
    squares = jnp.broadcast_to(jnp.sum(squares, axis=1, keepdims=True), (8, HD))
    squares = squares + pltpu.roll(squares, 4, 0)
    inv_rms = lax.rsqrt(squares * (1.0 / (HEADS * HD)) + 1e-05)
    scale8 = jnp.broadcast_to(inv_rms[None], (rows_all // 8, 8, HD))
    normed = mixed[...].reshape(rows_all // 8, 8, HD) * scale8 * wide32[...].reshape(rows_all // 8, 8, HD)
    nrm[...] = normed.reshape(rows_all, HD).astype(BF16).reshape(nrm.shape)

    pl.semaphore_wait(barrier, len(peers))
    for d in (2, 1, 3):
        send("n%d" % d, nrm.at[wrap(x + d)], abuf.at[x], X(d))
    keep = pltpu.make_async_copy(nrm.at[x], abuf.at[x], osem.at[0])
    keep.start()
    keep.wait()
    got("n1", "n2", "n3")
    block_rows = abuf.shape[1]
    block_heads = block_rows // seqs
    for n in range(4):
        wide32[pl.ds(n * block_rows, block_rows), :] = abuf[n].astype(F32)
    for n in range(4):
        for h in range(block_heads):
            stage[pl.ds(4 * n, 4), pl.ds(h * HD, HD)] = wide32[pl.ds(n * block_rows + 4 * h, 4), :]
    x_all[z, core, y] = stage[...].astype(BF16)

    def block(dz, dy):
        return x_all.at[wrap(z + dz), core, wrap(y + dy)]

    ops = {}

    def own():
        b = block(0, 0)
        send("y+a", b.at[:, lo], b.at[:, lo], Y(1))
        send("y-a", b.at[:, hi], b.at[:, hi], Y(-1))
        send("y+b", b.at[:, hi], b.at[:, hi], Y(1))
        send("y-b", b.at[:, lo], b.at[:, lo], Y(-1))
        send("s0", b, b, S)

    ops["own"] = own

    def over_z(r, tag):
        b = block(0, r)
        if r == 0:
            h = b.at[:, hi]
            send("q+", h, h, Z(1))
            send("q-", h, h, Z(-1))
        send("z+" + tag, b.at[:, lo], b.at[:, lo], Z(1))
        send("z-" + tag, b.at[:, lo], b.at[:, lo], Z(-1))
        if r == 0:
            send("q2", h, h, Z(2))
        else:
            send("s" + tag, b, b, S)

    def over_y(i, dep):
        got(dep)
        b = block(deltas[i], 0).at[:, hi]
        send("u%dm" % i, b, b, Y(1))
        send("u%dp" % i, b, b, Y(-1))
        send("u%d2" % i, b, b, Y(2))

    ops["yq1"] = lambda: over_y(1, "q-")
    ops["yq2"] = lambda: over_y(2, "q+")
    ops["yq3"] = lambda: over_y(3, "q2")

    ops["z0"] = lambda: over_z(0, "0")

    def yfm():
        got("y+a")
        b = block(0, -1).at[:, lo]
        send("yf+", b, b, Y(1))

    def yfp():
        got("y-a")
        b = block(0, 1).at[:, hi]
        send("yf-", b, b, Y(-1))

    def zm():
        got("y+b")
        over_z(-1, "m")

    def zp():
        got("y-b")
        over_z(1, "p")

    def z2():
        got("yf+", "yf-")
        over_z(2, "2")

    ops.update(yfm=yfm, yfp=yfp, zm=zm, zp=zp, z2=z2)

    def zf(sign, r, tag):
        d = "+" if sign > 0 else "-"
        got("z" + d + tag)
        b = block(-sign, r).at[:, lo]
        send("zf" + d + tag, b, b, Z(sign))

    ops["zfm0"] = lambda: zf(1, 0, "0")
    ops["zfmm"] = lambda: zf(1, -1, "m")
    ops["zfpp"] = lambda: zf(-1, 1, "p")
    ops["zfp2"] = lambda: zf(-1, 2, "2")

    def slab(k, *names):
        got(*names)
        got(*("u%d%s" % (k, t) for t in "mp2"))
        b = x_all.at[wrap(z + deltas[k]), core]
        send("sl%d" % k, b, b, S)

    ops["S1"] = lambda: slab(1, "q-", "z-0", "z-m", "z-p", "z-2")
    ops["S2"] = lambda: slab(2, "q+", "z+0", "z+m", "z+p", "z+2")
    ops["S3"] = lambda: slab(3, "q2", "zf+0", "zf+m", "zf-p", "zf-2")

    def gate_half(k):
        if k == 0:
            for c in loads:
                c.wait()
            got("s0", "sm", "sp", "s2")
        else:
            got("sl%d" % k)
        lhs = x_all[wrap(z + deltas[k])].reshape(128, x_all.shape[4])
        r = jnp.dot(lhs, wgu[0], preferred_element_type=F32).astype(BF16)
        part[k, 0] = r.reshape(4, 32, width)
        send("a%d" % k, part.at[k, 0, xp2], ra.at[k], X(1))
        send("d%d" % k, part.at[k, 0, xm1], rp.at[k, 0], X(-1))

    def up_half(k):
        lhs = x_all[wrap(z + deltas[k])].reshape(128, x_all.shape[4])
        r = jnp.dot(lhs, wgu[1], preferred_element_type=F32).astype(BF16)
        part[k, 1] = r.reshape(4, 32, width)
        send("b%d" % k, part.at[k, 1, xp2], rb.at[k], X(-1))
        send("c%d" % k, part.at[k, 1, xp1], rm.at[k, 1], X(1))

    def mid_a(k):
        got("a%d" % k)
        part[k, 0, xp1] = (part[k, 0, xp1].astype(F32) + ra[k].astype(F32)).astype(BF16)
        send("e%d" % k, part.at[k, 0, xp1], rm.at[k, 0], X(1))

    def mid_b(k):
        got("b%d" % k)
        part[k, 1, xm1] = (part[k, 1, xm1].astype(F32) + rb[k].astype(F32)).astype(BF16)
        send("f%d" % k, part.at[k, 1, xm1], rp.at[k, 1], X(-1))

    def gate(k):
        got("d%d" % k, "c%d" % k, "e%d" % k, "f%d" % k)
        for j in range(width // 128):
            cols = pl.ds(j * 128, 128)

            def total(h):
                return (part[k, h, x, :, cols].astype(F32) + rm[k, h, :, cols].astype(F32)
                        + rp[k, h, :, cols].astype(F32))

            hid[k, x, :, cols] = (jax.nn.silu(total(0)) * total(1)).astype(BF16)
        b = hid.at[k, x]
        send("h+%d" % k, b, b, X(1))
        send("h-%d" % k, b, b, X(-1))
        send("h2%d" % k, b, b, X(2))

    def down(k, h):
        if h == 0:
            if k == 0:
                for c in dloads:
                    c.wait()
            got("h+%d" % k, "h-%d" % k, "h2%d" % k)
        tiles = down_tiles // 2

        def step(n, carry):
            lhs = hid[k].reshape(128, width)
            r = jnp.dot(lhs, wd[h * tiles + n], preferred_element_type=F32).astype(BF16)
            at = pl.multiple_of(h * half + n * dn, dn)
            dpart[k, :, :, :, pl.ds(at, dn)] = r.reshape(2, 4, 16, dn)
            return carry

        lax.fori_loop(0, tiles, step, 0)
        cols = hi if h else lo
        send("EW"[h] + str(k), dpart.at[k, other, :, :, cols], sib.at[k, :, :, cols], S)

    def sib_add(k, h):
        got("EW"[h] + str(k))
        cols = hi if h else lo

        def step(i, carry):
            yi = lax.rem(yp2 + i, 4)
            dpart[k, core, yi, :, cols] = (
                dpart[k, core, yi, :, cols].astype(F32) + sib[k, yi, :, cols].astype(F32)).astype(BF16)
            return carry

        lax.fori_loop(0, 4, step, 0)
        if h == 0:
            send("t1%d" % k, dpart.at[k, core, yp2, :, lo], ya.at[k], Y(1))
            send("t4%d" % k, dpart.at[k, core, ym1, :, lo], yp.at[k, :, lo], Y(-1))
        else:
            send("t2%d" % k, dpart.at[k, core, yp2, :, hi], yb.at[k], Y(-1))
            send("t3%d" % k, dpart.at[k, core, yp1, :, hi], ym.at[k, :, hi], Y(1))

    def y_mid(k, h):
        if h == 0:
            got("t1%d" % k)
            dpart[k, core, yp1, :, lo] = (
                dpart[k, core, yp1, :, lo].astype(F32) + ya[k].astype(F32)).astype(BF16)
            send("t5%d" % k, dpart.at[k, core, yp1, :, lo], ym.at[k, :, lo], Y(1))
        else:
            got("t2%d" % k)
            dpart[k, core, ym1, :, hi] = (
                dpart[k, core, ym1, :, hi].astype(F32) + yb[k].astype(F32)).astype(BF16)
            send("t6%d" % k, dpart.at[k, core, ym1, :, hi], yp.at[k, :, hi], Y(-1))

    def y_fin(k, h):
        cols = hi if h else lo
        if h == 0:
            got("t4%d" % k, "t5%d" % k)
        else:
            got("t3%d" % k, "t6%d" % k)
        stage[:, cols] = (dpart[k, core, y, :, cols].astype(F32) + ym[k, :, cols].astype(F32)
                          + yp[k, :, cols].astype(F32))
        part_rows = block_rows // 2
        first = h * part_rows
        piece = pl.ds(first, part_rows)
        for n in range(4):
            for i in range(block_heads // 2):
                head = h * (block_heads // 2) + i
                wide32[pl.ds(n * block_rows + 4 * head, 4), :] = stage[pl.ds(4 * n, 4), pl.ds(head * HD, HD)]
            zs[k, n, piece, :] = wide32[pl.ds(n * block_rows + first, part_rows), :].astype(BF16)
        for dx in (2, 1, 3, 0):
            if dx == 0 and k == 0:
                keep = pltpu.make_async_copy(zs.at[k, x, piece], zr.at[k, x, piece], osem.at[1 + h])
                keep.start()
                keep.wait()
            else:
                send("v%d%d%d" % (k, dx, h), zs.at[k, wrap(x + dx), piece], zr.at[k, x, piece],
                     XZ(dx, deltas[k]))

    def finish():
        for k in range(4):
            got(*("v%d%d%d" % (k, dx, h) for dx in range(4) for h in range(2) if k or dx))
        for n in range(4):
            ffn = (zr[0, n].astype(F32) + zr[1, n].astype(F32) + zr[2, n].astype(F32)
                   + zr[3, n].astype(F32)).astype(BF16)
            rows = pl.ds(n * block_rows, block_rows)
            out[rows, :] = mixed[rows, :] + ffn.astype(F32)

    for k in range(4):
        n = str(k)
        ops["G" + n] = functools.partial(gate_half, k)
        ops["U" + n] = functools.partial(up_half, k)
        ops["rA" + n] = functools.partial(mid_a, k)
        ops["rB" + n] = functools.partial(mid_b, k)
        ops["gate" + n] = functools.partial(gate, k)
        ops["D" + n] = functools.partial(down, k, 0)
        ops["V" + n] = functools.partial(down, k, 1)
        ops["A" + n] = functools.partial(sib_add, k, 0)
        ops["B" + n] = functools.partial(sib_add, k, 1)
        ops["yA" + n] = functools.partial(y_mid, k, 0)
        ops["yB" + n] = functools.partial(y_mid, k, 1)
        ops["yL" + n] = functools.partial(y_fin, k, 0)
        ops["yH" + n] = functools.partial(y_fin, k, 1)
    ops["end"] = finish

    for name in ORDER:
        ops[name]()
    for i, (members, ref) in enumerate(send_groups):
        assert set(members) <= set(started)
        sum_of(ref, i, 0).wait_send()


def by_head(a):
    rows, cols = a.shape
    return a.reshape(rows, HEADS, HD).transpose(1, 0, 2).reshape(rows * HEADS, HD)


def body(
    resid,
    queries,
    key_cache,
    value_cache,
    new_keys,
    new_values,
    lengths,
    norm_gain,
    w_gate,
    w_up,
    w_down,
):
    depth, width = w_gate.shape
    cols = w_down.shape[1]
    seqs, cached, kv = key_cache.shape
    rows = seqs * HEADS
    dn = 1024
    down_tiles = cols // dn
    b16 = functools.partial(pltpu.VMEM, dtype=BF16)
    out = pl.pallas_call(
        layer_kernel,
        out_shape=jax.ShapeDtypeStruct((rows, HD), F32),
        in_specs=[pl.BlockSpec(memory_space=pl.ANY)] * 11,
        out_specs=pl.BlockSpec(memory_space=pltpu.VMEM),
        scratch_shapes=[
            pltpu.SMEM((seqs,), jnp.int32),
            b16((seqs, kv)),
            b16((seqs, kv)),
            b16((HEADS, HD)),
            b16((rows, HD)),
            b16((rows, HD)),
            b16((seqs, cached, kv)),
            b16((seqs, cached, kv)),
            b16((16, 2 * kv)),
            pltpu.VMEM((rows // KVH, seqs * cached), F32),
            pltpu.VMEM((rows, HD), F32),
            pltpu.VMEM((rows, HD), F32),
            b16((4, rows // 4, HD)),
            b16((2, depth, width)),
            b16((down_tiles, width, dn)),
            b16((4, rows // 4, HD)),
            pltpu.VMEM((16, depth), F32),
            b16((4, 2, 4, 16, depth)),
            b16((4, 2, 4, 32, width)),
            b16((4, 32, width)),
            b16((4, 32, width)),
            b16((4, 2, 32, width)),
            b16((4, 2, 32, width)),
            b16((4, 4, 32, width)),
            b16((4, 2, 4, 16, cols)),
            b16((4, 4, 16, cols)),
            b16((4, 16, cols // 2)),
            b16((4, 16, cols // 2)),
            b16((4, 16, cols)),
            b16((4, 16, cols)),
            b16((4, 4, rows // 4, HD)),
            b16((4, 4, rows // 4, HD)),
            pltpu.SemaphoreType.DMA((4, seqs)),
            pltpu.SemaphoreType.DMA((2 + down_tiles,)),
            pltpu.SemaphoreType.DMA((3,)),
            pltpu.SemaphoreType.DMA((DEPARTURES,)),
            pltpu.SemaphoreType.DMA((ARRIVALS,)),
        ],
        compiler_params=pltpu.CompilerParams(
            collective_id=0, has_side_effects=True, vmem_limit_bytes=58 * 1024 * 1024),
        name="layer",
    )(lengths, new_keys, new_values, norm_gain.reshape(HEADS, HD), by_head(queries), by_head(resid),
      key_cache, value_cache, w_gate, w_up, w_down)
    return out.astype(BF16).reshape(HEADS, seqs, HD).transpose(1, 0, 2).reshape(seqs, HEADS * HD)


def solution(mesh):
    return jax.shard_map(
        body,
        mesh=mesh,
        in_specs=(
            P(("wide", "narrow"), None),
            P(("wide", "narrow"), None),
            P(("wide", "narrow"), None, None),
            P(("wide", "narrow"), None, None),
            P(("wide", "narrow"), None),
            P(("wide", "narrow"), None),
            P(("wide", "narrow")),
            P(),
            P("narrow", "wide"),
            P("narrow", "wide"),
            P("wide", "narrow"),
        ),
        out_specs=P(("wide", "narrow"), None),
        check_vma=False,
    )
```

```python
import functools

import jax
import jax.numpy as jnp
from jax import lax
from jax.experimental import pallas as pl
from jax.experimental.pallas import tpu as pltpu
from jax.sharding import PartitionSpec as P

HEADS = 128
KVH = 8
HD = 128
MESH = pl.DeviceIdType.MESH
F32 = jnp.float32
BF16 = jnp.bfloat16
ARRIVALS = 67
DEPARTURES = 15
ORDER = (
    "own", "z0", "yfm", "yfp", "yq1", "yq2", "zm", "zp",
    "z2", "G0", "U0", "zfm0", "zfmm", "zfpp", "zfp2", "yq3",
    "S1", "S2", "rA0", "rB0", "G1", "U1", "G2", "U2",
    "S3", "gate0", "rA1", "rB1", "G3", "U3", "D0", "rB2",
    "rA2", "V0", "gate1", "rA3", "B0", "A0", "rB3", "gate2",
    "D1", "V1", "yA0", "yB0", "gate3", "A1", "D2", "B1",
    "V2", "A2", "D3", "B2", "yB1", "yA1", "V3", "A3",
    "yA2", "B3", "yB2", "yH0", "yL0", "yH1", "yA3", "yL1",
    "yL2", "yB3", "yH2", "yL3", "yH3", "end",
)


def scaled_scores(q, k):
    return lax.dot_general(q, k, (((1,), (1,)), ((), ())), preferred_element_type=F32) * (1.0 / HD**0.5)


def layer_kernel(
    lens_hbm, nk_hbm, nv_hbm, gain_hbm, q_hbm, resid_hbm, k_hbm, v_hbm, wg_hbm, wu_hbm, wd_hbm,
    out,
    lens, nk, nv, gain, q, resid, kc, vc, nkv, bias, mixed, wide32, nrm,
    wgu, wd, abuf, stage, x_all,
    part, ra, rb, rm, rp, hid,
    dpart, sib, ya, yb, ym, yp, zs, zr,
    isem, wsem, osem, ss, rs,
):
    x = lax.axis_index("narrow")
    w = lax.axis_index("wide")
    z = lax.div(w, 8)
    y = lax.rem(lax.div(w, 2), 4)
    core = lax.rem(w, 2)
    other = 1 - core

    def wrap(v):
        return lax.rem(v + 4, 4)

    def X(d):
        return {"narrow": wrap(x + d)}

    def Y(d):
        return {"wide": z * 8 + wrap(y + d) * 2 + core}

    def Z(d):
        return {"wide": wrap(z + d) * 8 + y * 2 + core}

    def XZ(dx, dz):
        if dz == 0:
            return X(dx)
        if dx == 0:
            return Z(dz)
        return {"narrow": wrap(x + dx), "wide": wrap(z + dz) * 8 + y * 2 + core}

    S = {"wide": w + 1 - 2 * core}
    xp1, xm1, xp2 = wrap(x + 1), wrap(x - 1), wrap(x + 2)
    yp1, ym1, yp2 = wrap(y + 1), wrap(y - 1), wrap(y + 2)
    deltas = (0, 1, -1, 2)

    half = x_all.shape[4] // 2
    lo = pl.ds(0, half)
    hi = pl.ds(half, half)
    halves = x_all.at[0, 0, :, :, lo]
    recv_groups = [
        (("s0", "sm", "sp", "s2"), sib.at[0]),
        (("yf+", "yf-"), ym.at[0]),
        (("z-0", "z-m"), ym.at[0]),
        (("z+p", "z+2"), ym.at[0]),
        (("zf+0", "zf+m", "zf-p", "zf-2"), halves),
        (("n1", "n2", "n3"), nrm.at[pl.ds(0, 3)]),
    ]
    send_groups = [
        (("n1", "n2", "n3"), nrm.at[pl.ds(0, 3)]),
        (tuple("h2%d" % k for k in range(4)), hid.at[0]),
        (tuple(t + str(k) for k in range(4) for t in "EW"), sib),
        (tuple("t%d%d" % (t, k) for k in range(4) for t in range(1, 7)), sib.at[pl.ds(0, 3)]),
        (("s0", "sm", "sp", "s2", "sl1", "sl2", "sl3"), sib),
        (("y+a", "y-a", "y+b", "y-b", "yf+", "yf-"), sib.at[0, pl.ds(0, 3)]),
        (("z+0", "z-0", "z+m", "z-m", "z+p", "z-p", "z+2", "z-2", "zf+0", "zf+m", "zf-p", "zf-2", "q+", "q-",
          "q2") + tuple("u%d%s" % (k, t) for k in (1, 2, 3) for t in "mp2"), sib.at[pl.ds(0, 3)]),
    ]
    for k in range(4):
        if k:
            recv_groups.append((tuple("u%d%s" % (k, t) for t in "mp2"), x_all.at[0, 0, pl.ds(0, 3), :, lo]))
        recv_groups.append((tuple(t + str(k) for t in "cdef"), hid.at[k]))
        recv_groups.append((tuple("h%s%d" % (t, k) for t in "+-2"), hid.at[k, pl.ds(0, 3)]))
        recv_groups.append((("t4%d" % k, "t5%d" % k), ym.at[k]))
        recv_groups.append((("t3%d" % k, "t6%d" % k), ym.at[k]))
        send_groups.append((tuple(t + str(k) for t in "abcdef") + ("h+%d" % k, "h-%d" % k), part.at[k]))
        pieces = tuple("v%d%d%d" % (k, dx, h) for dx in range(4) for h in range(2) if k or dx)
        ref = zs.at[k] if k else zs.at[0, pl.ds(0, 3)]
        recv_groups.append((pieces, ref))
        send_groups.append((pieces, ref))
    recv_of = {n: i for i, g in enumerate(recv_groups) for n in g[0]}
    send_of = {n: i for i, g in enumerate(send_groups) for n in g[0]}

    count = [len(recv_groups)]
    started = []
    arrived = set()
    cp = {}

    def send(name, src, dst, dev):
        i = recv_of.get(name)
        if i is None:
            i = count[0]
            count[0] += 1
        c = pltpu.make_async_remote_copy(
            src_ref=src, dst_ref=dst, send_sem=ss.at[send_of[name]], recv_sem=rs.at[i],
            device_id=dev, device_id_type=MESH)
        started.append(name)
        c.start()
        cp[name] = c

    def sum_of(ref, i, j):
        return pltpu.make_async_remote_copy(
            src_ref=ref, dst_ref=ref, send_sem=ss.at[i], recv_sem=rs.at[j], device_id=X(1), device_id_type=MESH)

    def got(*names):
        for n in names:
            if n in arrived:
                continue
            if n in recv_of:
                members, ref = recv_groups[recv_of[n]]
                assert set(members) <= set(names) and set(members) <= set(started)
                sum_of(ref, 0, recv_of[n]).wait_recv()
                arrived.update(members)
            else:
                cp[n].wait_recv()
                arrived.add(n)

    seqs, cached = kc.shape[0], kc.shape[1]
    early = [pltpu.make_async_copy(q_hbm, q, isem.at[0, 0])]
    early += [pltpu.make_async_copy(k_hbm.at[b], kc.at[b], isem.at[1, b]) for b in range(seqs)]
    early += [pltpu.make_async_copy(v_hbm.at[b], vc.at[b], isem.at[2, b]) for b in range(seqs)]
    small = [
        pltpu.make_async_copy(lens_hbm, lens, isem.at[3, 0]),
        pltpu.make_async_copy(nk_hbm, nk, isem.at[3, 1]),
        pltpu.make_async_copy(nv_hbm, nv, isem.at[3, 2]),
        pltpu.make_async_copy(gain_hbm, gain, isem.at[3, 3]),
    ]
    late = pltpu.make_async_copy(resid_hbm, resid, isem.at[0, 1])
    early.append(late)
    for c in small + early:
        c.start()

    barrier = pltpu.get_barrier_semaphore()
    peers = [XZ(dx, dz) for dx in range(4) for dz in range(4) if (dx, dz) != (0, 0)]
    peers += [Y(1), Y(2), Y(3), S]
    for p in peers:
        pl.semaphore_signal(barrier, inc=1, device_id=p, device_id_type=MESH)

    group_rows = q.shape[0] // KVH
    shape = (group_rows, seqs * cached)
    row_seq = lax.broadcasted_iota(jnp.int32, shape, 0) & 3
    col = lax.broadcasted_iota(jnp.int32, shape, 1)
    col_seq = jnp.zeros(shape, jnp.int32)
    for b in range(1, seqs):
        col_seq = col_seq + (col >= b * cached).astype(jnp.int32)
    rows_all = q.shape[0]
    pick = ((lax.broadcasted_iota(jnp.int32, (rows_all, HEADS), 0) >> 2)
            == lax.broadcasted_iota(jnp.int32, (rows_all, HEADS), 1))
    pick = jnp.where(pick, F32(1.0), F32(0.0)).astype(BF16)
    own_seq = (lax.broadcasted_iota(jnp.int32, (group_rows, 16), 0) & 3) == lax.broadcasted_iota(
        jnp.int32, (group_rows, 16), 1)
    stage[...] = jnp.zeros_like(stage)
    for c in small:
        c.wait()
    limit = jnp.zeros(shape, jnp.int32)
    for b in range(seqs):
        limit = jnp.where(row_seq == b, lens[b] + b * cached, limit)
    bias[...] = jnp.where((col_seq == row_seq) & (col < limit), F32(0.0), F32(-1e30))
    width_kv = nk.shape[1]
    stage[pl.ds(0, 4), pl.ds(0, width_kv)] = nk[...].astype(F32)
    stage[pl.ds(0, 4), pl.ds(width_kv, width_kv)] = nv[...].astype(F32)
    nkv[...] = stage[:, pl.ds(0, 2 * width_kv)].astype(BF16)
    wide32[...] = jnp.dot(pick, gain[...], preferred_element_type=F32)

    for c in early:
        c.wait()

    down_tiles = wd.shape[0]
    dn = wd.shape[2]
    width = wgu.shape[2]
    loads = [
        pltpu.make_async_copy(wg_hbm, wgu.at[0], wsem.at[0]),
        pltpu.make_async_copy(wu_hbm, wgu.at[1], wsem.at[1]),
    ]
    dloads = []
    for n in range(down_tiles):
        dloads.append(pltpu.make_async_copy(
            wd_hbm.at[:, pl.ds(n * dn, dn)], wd.at[n], wsem.at[2 + n]))
    for c in loads:
        c.start()
    for c in dloads:
        c.start()

    def attend(g, carry):
        rows = pl.ds(pl.multiple_of(g * group_rows, group_rows), group_rows)
        lanes = pl.ds(pl.multiple_of(g * HD, HD), HD)
        vlanes = pl.ds(pl.multiple_of(width_kv + g * HD, HD), HD)
        qg = q[rows, :]
        scores = scaled_scores(qg, kc[:, :, lanes].reshape(seqs * cached, HD)) + bias[...]
        own = scaled_scores(qg, nkv[:, lanes])
        own = jnp.sum(jnp.where(own_seq, own, F32(0.0)), axis=1, keepdims=True)
        top = jnp.maximum(jnp.max(scores, axis=1, keepdims=True), own)
        cache_exp = jnp.exp(scores - top)
        own_exp = jnp.exp(own - top)
        inverse = 1.0 / (jnp.sum(cache_exp, axis=1, keepdims=True) + own_exp)
        probs = (cache_exp * inverse).astype(BF16)
        own_prob = jnp.where(own_seq, own_exp * inverse, F32(0.0)).astype(BF16)
        attended = jnp.dot(probs, vc[:, :, lanes].reshape(seqs * cached, HD), preferred_element_type=F32)
        attended = attended + jnp.dot(own_prob, nkv[:, vlanes], preferred_element_type=F32)
        m = resid[rows, :].astype(F32) + attended
        mixed[rows, :] = m
        return carry + jnp.sum((m * m).reshape(group_rows // 8, 8, HD), axis=0)

    squares = lax.fori_loop(0, KVH, attend, jnp.zeros((8, HD), F32), unroll=True)
    squares = jnp.broadcast_to(jnp.sum(squares, axis=1, keepdims=True), (8, HD))
    squares = squares + pltpu.roll(squares, 4, 0)
    inv_rms = lax.rsqrt(squares * (1.0 / (HEADS * HD)) + 1e-05)
    scale8 = jnp.broadcast_to(inv_rms[None], (rows_all // 8, 8, HD))
    normed = mixed[...].reshape(rows_all // 8, 8, HD) * scale8 * wide32[...].reshape(rows_all // 8, 8, HD)
    nrm[...] = normed.reshape(rows_all, HD).astype(BF16).reshape(nrm.shape)

    pl.semaphore_wait(barrier, len(peers))
    for d in (2, 1, 3):
        send("n%d" % d, nrm.at[wrap(x + d)], abuf.at[x], X(d))
    keep = pltpu.make_async_copy(nrm.at[x], abuf.at[x], osem.at[0])
    keep.start()
    keep.wait()
    got("n1", "n2", "n3")
    block_rows = abuf.shape[1]
    block_heads = block_rows // seqs
    for n in range(4):
        wide32[pl.ds(n * block_rows, block_rows), :] = abuf[n].astype(F32)
    for n in range(4):
        for h in range(block_heads):
            stage[pl.ds(4 * n, 4), pl.ds(h * HD, HD)] = wide32[pl.ds(n * block_rows + 4 * h, 4), :]
    x_all[z, core, y] = stage[...].astype(BF16)

    def block(dz, dy):
        return x_all.at[wrap(z + dz), core, wrap(y + dy)]

    ops = {}

    def own():
        b = block(0, 0)
        send("y+a", b.at[:, lo], b.at[:, lo], Y(1))
        send("y-a", b.at[:, hi], b.at[:, hi], Y(-1))
        send("y+b", b.at[:, hi], b.at[:, hi], Y(1))
        send("y-b", b.at[:, lo], b.at[:, lo], Y(-1))
        send("s0", b, b, S)

    ops["own"] = own

    def over_z(r, tag):
        b = block(0, r)
        if r == 0:
            h = b.at[:, hi]
            send("q+", h, h, Z(1))
            send("q-", h, h, Z(-1))
        send("z+" + tag, b.at[:, lo], b.at[:, lo], Z(1))
        send("z-" + tag, b.at[:, lo], b.at[:, lo], Z(-1))
        if r == 0:
            send("q2", h, h, Z(2))
        else:
            send("s" + tag, b, b, S)

    def over_y(i, dep):
        got(dep)
        b = block(deltas[i], 0).at[:, hi]
        send("u%dm" % i, b, b, Y(1))
        send("u%dp" % i, b, b, Y(-1))
        send("u%d2" % i, b, b, Y(2))

    ops["yq1"] = lambda: over_y(1, "q-")
    ops["yq2"] = lambda: over_y(2, "q+")
    ops["yq3"] = lambda: over_y(3, "q2")

    ops["z0"] = lambda: over_z(0, "0")

    def yfm():
        got("y+a")
        b = block(0, -1).at[:, lo]
        send("yf+", b, b, Y(1))

    def yfp():
        got("y-a")
        b = block(0, 1).at[:, hi]
        send("yf-", b, b, Y(-1))

    def zm():
        got("y+b")
        over_z(-1, "m")

    def zp():
        got("y-b")
        over_z(1, "p")

    def z2():
        got("yf+", "yf-")
        over_z(2, "2")

    ops.update(yfm=yfm, yfp=yfp, zm=zm, zp=zp, z2=z2)

    def zf(sign, r, tag):
        d = "+" if sign > 0 else "-"
        got("z" + d + tag)
        b = block(-sign, r).at[:, lo]
        send("zf" + d + tag, b, b, Z(sign))

    ops["zfm0"] = lambda: zf(1, 0, "0")
    ops["zfmm"] = lambda: zf(1, -1, "m")
    ops["zfpp"] = lambda: zf(-1, 1, "p")
    ops["zfp2"] = lambda: zf(-1, 2, "2")

    def slab(k, *names):
        got(*names)
        got(*("u%d%s" % (k, t) for t in "mp2"))
        b = x_all.at[wrap(z + deltas[k]), core]
        send("sl%d" % k, b, b, S)

    ops["S1"] = lambda: slab(1, "q-", "z-0", "z-m", "z-p", "z-2")
    ops["S2"] = lambda: slab(2, "q+", "z+0", "z+m", "z+p", "z+2")
    ops["S3"] = lambda: slab(3, "q2", "zf+0", "zf+m", "zf-p", "zf-2")

    def gate_half(k):
        if k == 0:
            for c in loads:
                c.wait()
            got("s0", "sm", "sp", "s2")
        else:
            got("sl%d" % k)
        lhs = x_all[wrap(z + deltas[k])].reshape(128, x_all.shape[4])
        r = jnp.dot(lhs, wgu[0], preferred_element_type=F32).astype(BF16)
        part[k, 0] = r.reshape(4, 32, width)
        send("a%d" % k, part.at[k, 0, xp2], ra.at[k], X(1))
        send("d%d" % k, part.at[k, 0, xm1], rp.at[k, 0], X(-1))

    def up_half(k):
        lhs = x_all[wrap(z + deltas[k])].reshape(128, x_all.shape[4])
        r = jnp.dot(lhs, wgu[1], preferred_element_type=F32).astype(BF16)
        part[k, 1] = r.reshape(4, 32, width)
        send("b%d" % k, part.at[k, 1, xp2], rb.at[k], X(-1))
        send("c%d" % k, part.at[k, 1, xp1], rm.at[k, 1], X(1))

    def mid_a(k):
        got("a%d" % k)
        part[k, 0, xp1] = (part[k, 0, xp1].astype(F32) + ra[k].astype(F32)).astype(BF16)
        send("e%d" % k, part.at[k, 0, xp1], rm.at[k, 0], X(1))

    def mid_b(k):
        got("b%d" % k)
        part[k, 1, xm1] = (part[k, 1, xm1].astype(F32) + rb[k].astype(F32)).astype(BF16)
        send("f%d" % k, part.at[k, 1, xm1], rp.at[k, 1], X(-1))

    def gate(k):
        got("d%d" % k, "c%d" % k, "e%d" % k, "f%d" % k)
        for j in range(width // 128):
            cols = pl.ds(j * 128, 128)

            def total(h):
                return (part[k, h, x, :, cols].astype(F32) + rm[k, h, :, cols].astype(F32)
                        + rp[k, h, :, cols].astype(F32))

            hid[k, x, :, cols] = (jax.nn.silu(total(0)) * total(1)).astype(BF16)
        b = hid.at[k, x]
        send("h+%d" % k, b, b, X(1))
        send("h-%d" % k, b, b, X(-1))
        send("h2%d" % k, b, b, X(2))

    def down(k, h):
        if h == 0:
            if k == 0:
                for c in dloads:
                    c.wait()
            got("h+%d" % k, "h-%d" % k, "h2%d" % k)
        tiles = down_tiles // 2

        def step(n, carry):
            lhs = hid[k].reshape(128, width)
            r = jnp.dot(lhs, wd[h * tiles + n], preferred_element_type=F32).astype(BF16)
            at = pl.multiple_of(h * half + n * dn, dn)
            dpart[k, :, :, :, pl.ds(at, dn)] = r.reshape(2, 4, 16, dn)
            return carry

        lax.fori_loop(0, tiles, step, 0)
        cols = hi if h else lo
        send("EW"[h] + str(k), dpart.at[k, other, :, :, cols], sib.at[k, :, :, cols], S)

    def sib_add(k, h):
        got("EW"[h] + str(k))
        cols = hi if h else lo

        def step(i, carry):
            yi = lax.rem(yp2 + i, 4)
            dpart[k, core, yi, :, cols] = (
                dpart[k, core, yi, :, cols].astype(F32) + sib[k, yi, :, cols].astype(F32)).astype(BF16)
            return carry

        lax.fori_loop(0, 4, step, 0)
        if h == 0:
            send("t1%d" % k, dpart.at[k, core, yp2, :, lo], ya.at[k], Y(1))
            send("t4%d" % k, dpart.at[k, core, ym1, :, lo], yp.at[k, :, lo], Y(-1))
        else:
            send("t2%d" % k, dpart.at[k, core, yp2, :, hi], yb.at[k], Y(-1))
            send("t3%d" % k, dpart.at[k, core, yp1, :, hi], ym.at[k, :, hi], Y(1))

    def y_mid(k, h):
        if h == 0:
            got("t1%d" % k)
            dpart[k, core, yp1, :, lo] = (
                dpart[k, core, yp1, :, lo].astype(F32) + ya[k].astype(F32)).astype(BF16)
            send("t5%d" % k, dpart.at[k, core, yp1, :, lo], ym.at[k, :, lo], Y(1))
        else:
            got("t2%d" % k)
            dpart[k, core, ym1, :, hi] = (
                dpart[k, core, ym1, :, hi].astype(F32) + yb[k].astype(F32)).astype(BF16)
            send("t6%d" % k, dpart.at[k, core, ym1, :, hi], yp.at[k, :, hi], Y(-1))

    def y_fin(k, h):
        cols = hi if h else lo
        if h == 0:
            got("t4%d" % k, "t5%d" % k)
        else:
            got("t3%d" % k, "t6%d" % k)
        stage[:, cols] = (dpart[k, core, y, :, cols].astype(F32) + ym[k, :, cols].astype(F32)
                          + yp[k, :, cols].astype(F32))
        part_rows = block_rows // 2
        first = h * part_rows
        piece = pl.ds(first, part_rows)
        for n in range(4):
            for i in range(block_heads // 2):
                head = h * (block_heads // 2) + i
                wide32[pl.ds(n * block_rows + 4 * head, 4), :] = stage[pl.ds(4 * n, 4), pl.ds(head * HD, HD)]
            zs[k, n, piece, :] = wide32[pl.ds(n * block_rows + first, part_rows), :].astype(BF16)
        for dx in (2, 1, 3, 0):
            if dx == 0 and k == 0:
                keep = pltpu.make_async_copy(zs.at[k, x, piece], zr.at[k, x, piece], osem.at[1 + h])
                keep.start()
                keep.wait()
            else:
                send("v%d%d%d" % (k, dx, h), zs.at[k, wrap(x + dx), piece], zr.at[k, x, piece],
                     XZ(dx, deltas[k]))

    def finish():
        for k in range(4):
            got(*("v%d%d%d" % (k, dx, h) for dx in range(4) for h in range(2) if k or dx))
        for n in range(4):
            ffn = (zr[0, n].astype(F32) + zr[1, n].astype(F32) + zr[2, n].astype(F32)
                   + zr[3, n].astype(F32)).astype(BF16)
            rows = pl.ds(n * block_rows, block_rows)
            out[rows, :] = mixed[rows, :] + ffn.astype(F32)

    for k in range(4):
        n = str(k)
        ops["G" + n] = functools.partial(gate_half, k)
        ops["U" + n] = functools.partial(up_half, k)
        ops["rA" + n] = functools.partial(mid_a, k)
        ops["rB" + n] = functools.partial(mid_b, k)
        ops["gate" + n] = functools.partial(gate, k)
        ops["D" + n] = functools.partial(down, k, 0)
        ops["V" + n] = functools.partial(down, k, 1)
        ops["A" + n] = functools.partial(sib_add, k, 0)
        ops["B" + n] = functools.partial(sib_add, k, 1)
        ops["yA" + n] = functools.partial(y_mid, k, 0)
        ops["yB" + n] = functools.partial(y_mid, k, 1)
        ops["yL" + n] = functools.partial(y_fin, k, 0)
        ops["yH" + n] = functools.partial(y_fin, k, 1)
    ops["end"] = finish

    for name in ORDER:
        ops[name]()
    for i, (members, ref) in enumerate(send_groups):
        assert set(members) <= set(started)
        sum_of(ref, i, 0).wait_send()


def by_head(a):
    rows, cols = a.shape
    return a.reshape(rows, HEADS, HD).transpose(1, 0, 2).reshape(rows * HEADS, HD)


def body(
    resid,
    queries,
    key_cache,
    value_cache,
    new_keys,
    new_values,
    lengths,
    norm_gain,
    w_gate,
    w_up,
    w_down,
):
    depth, width = w_gate.shape
    cols = w_down.shape[1]
    seqs, cached, kv = key_cache.shape
    rows = seqs * HEADS
    dn = 1024
    down_tiles = cols // dn
    b16 = functools.partial(pltpu.VMEM, dtype=BF16)
    out = pl.pallas_call(
        layer_kernel,
        out_shape=jax.ShapeDtypeStruct((rows, HD), F32),
        in_specs=[pl.BlockSpec(memory_space=pl.ANY)] * 11,
        out_specs=pl.BlockSpec(memory_space=pltpu.VMEM),
        scratch_shapes=[
            pltpu.SMEM((seqs,), jnp.int32),
            b16((seqs, kv)),
            b16((seqs, kv)),
            b16((HEADS, HD)),
            b16((rows, HD)),
            b16((rows, HD)),
            b16((seqs, cached, kv)),
            b16((seqs, cached, kv)),
            b16((16, 2 * kv)),
            pltpu.VMEM((rows // KVH, seqs * cached), F32),
            pltpu.VMEM((rows, HD), F32),
            pltpu.VMEM((rows, HD), F32),
            b16((4, rows // 4, HD)),
            b16((2, depth, width)),
            b16((down_tiles, width, dn)),
            b16((4, rows // 4, HD)),
            pltpu.VMEM((16, depth), F32),
            b16((4, 2, 4, 16, depth)),
            b16((4, 2, 4, 32, width)),
            b16((4, 32, width)),
            b16((4, 32, width)),
            b16((4, 2, 32, width)),
            b16((4, 2, 32, width)),
            b16((4, 4, 32, width)),
            b16((4, 2, 4, 16, cols)),
            b16((4, 4, 16, cols)),
            b16((4, 16, cols // 2)),
            b16((4, 16, cols // 2)),
            b16((4, 16, cols)),
            b16((4, 16, cols)),
            b16((4, 4, rows // 4, HD)),
            b16((4, 4, rows // 4, HD)),
            pltpu.SemaphoreType.DMA((4, seqs)),
            pltpu.SemaphoreType.DMA((2 + down_tiles,)),
            pltpu.SemaphoreType.DMA((3,)),
            pltpu.SemaphoreType.DMA((DEPARTURES,)),
            pltpu.SemaphoreType.DMA((ARRIVALS,)),
        ],
        compiler_params=pltpu.CompilerParams(
            collective_id=0, has_side_effects=True, vmem_limit_bytes=58 * 1024 * 1024),
        name="layer",
    )(lengths, new_keys, new_values, norm_gain.reshape(HEADS, HD), by_head(queries), by_head(resid),
      key_cache, value_cache, w_gate, w_up, w_down)
    return out.astype(BF16).reshape(HEADS, seqs, HD).transpose(1, 0, 2).reshape(seqs, HEADS * HD)


def solution(mesh):
    return jax.shard_map(
        body,
        mesh=mesh,
        in_specs=(
            P(("wide", "narrow"), None),
            P(("wide", "narrow"), None),
            P(("wide", "narrow"), None, None),
            P(("wide", "narrow"), None, None),
            P(("wide", "narrow"), None),
            P(("wide", "narrow"), None),
            P(("wide", "narrow")),
            P(),
            P("narrow", "wide"),
            P("narrow", "wide"),
            P("wide", "narrow"),
        ),
        out_specs=P(("wide", "narrow"), None),
        check_vma=False,
    )
```
